32 devices in a mesh: seq: 8 (over y, x, core), emb: 4 (over z).
Axes of the slice: x: 2, y: 2, z: 4, core: 2. Of those that a mesh axis runs over, the one named last changes fastest.
Arguments:
- item_ids: int32 [16384], P('seq'), may hold values from 0 to 32767
- domains: int32 [16384], P(('seq', 'emb')), may hold values from 0 to 3, as said below
- live_counts: int32 [32], P(('seq', 'emb')), may hold values from 128 to 512, as said below
- table: bfloat16 [32768, 512], P(None, 'emb'), may hold values from -30 to 30
- norm_gains: float32 [3, 512], replicated, may hold values from 0.25 to 1.75
- proj_in: bfloat16 [512, 2048], replicated, may hold values from -0.25 to 0.25
- proj_out: bfloat16 [512, 512], replicated, may hold values from -0.25 to 0.25
- expert_in: bfloat16 [4, 512, 4096], P('emb'), may hold values from -0.25 to 0.25
- expert_out: bfloat16 [4, 2048, 512], P('emb'), may hold values from -0.125 to 0.125
Outputs:
- mixed: bfloat16 [16384, 512], P(('seq', 'emb'))
The draws below stay inside these ranges and needn't reach their ends.
Inputs may be any that keep to these rules, and one draw needn't show every extreme that they name: `domains`: in the 512 events of one block no domain appears more than 256 times; in every group of 4 consecutive blocks some domain appears exactly 256 times in each block. `live_counts`: some block has all 512 events live.
All inputs are finite; a program needn't handle non-finite values.
Results may differ from the reference program's by a relative error of at most 0.006.
Values may be sent and summed in bfloat16 or wider, within the bound.
No kernel may reach another device: no remote copies, remote signals or barrier semaphores. Data moves between devices by JAX's collectives and lax.ppermute only.
A program may use at most 128 MiB of HBM per device.

```python
import math
import jax
import jax.numpy as jnp
import numpy as np
from jax import lax

D = 512
HEADS = 8
HEAD_DIM = 64
HID = 2048
VOCAB = 32768
ROWS = 512
SPAN = 4
EXPERTS = 4
CAP = 256
EVENTS = 16384


def draw_domains(key, part):
    blocks = EVENTS // ROWS
    groups = blocks // EXPERTS
    first, second, third = jax.random.split(jax.random.fold_in(key, 11), 3)
    hot_group = jax.random.randint(first, (groups,), 0, EXPERTS)
    hot = jnp.repeat(hot_group, EXPERTS)
    second_off = jax.random.randint(second, (blocks, 1), 1, EXPERTS)
    remaining = ROWS - CAP
    paired = min(CAP, remaining) // 2
    places = jnp.arange(ROWS, dtype=jnp.int32)[None, :]
    cyclic = 1 + jnp.mod(places - CAP - paired, EXPERTS - 1)
    offset = jnp.where(places < CAP, 0, jnp.where(places < CAP + paired, second_off, cyclic))
    labels = jnp.mod(hot[:, None] + offset, EXPERTS)
    scores = jax.random.randint(third, (blocks, ROWS), 0, 1 << 20) * ROWS + places
    order = jnp.argsort(scores, axis=1, stable=True)
    labels = jnp.take_along_axis(labels, order, axis=1)
    return labels.reshape(EVENTS).astype(jnp.int32)


def draw_live_counts(key, part):
    blocks = EVENTS // ROWS
    first, second = jax.random.split(jax.random.fold_in(key, 23), 2)
    counts = jax.random.randint(first, (blocks,), ROWS // 4, ROWS + 1)
    chosen = jax.random.randint(second, (), 0, blocks)
    counts = jnp.where(jnp.arange(blocks) == chosen, ROWS, counts)
    return counts.astype(jnp.int32)


def draw_table(key, part):
    first, second, third = jax.random.split(jax.random.fold_in(key, 37), 3)
    row_scale = jnp.exp(jax.random.uniform(first, (VOCAB, 1), jnp.float32, math.log(0.3), math.log(3.0)))
    col_scale = jnp.exp(jax.random.uniform(second, (1, D), jnp.float32, math.log(0.5), math.log(2.0)))
    base = jnp.clip(jax.random.normal(third, (VOCAB, D), jnp.float32), -5.0, 5.0)
    return (base * row_scale * col_scale).astype(jnp.bfloat16)


def touch_ends(result, key, least, high):
    shape = result.shape
    spot = [jax.random.randint(jax.random.fold_in(key, axis), (), 0, shape[axis]) for axis in range(len(shape))]
    result = result.at[tuple(spot)].set(least)
    longest = shape.index(max(shape))
    spot[longest] = (spot[longest] + 1) % shape[longest]
    return result.at[tuple(spot)].set(high)


def shard_levels(rng, shape, cuts, low, largest):
    factor_of, own = 1.0, jax.random.fold_in(rng, 6)
    for axis_at, shards_of in cuts:
        steps = jnp.exp(jax.random.uniform(jax.random.fold_in(own, axis_at), (shards_of,), jnp.float32, low / len(cuts), largest / len(cuts)))
        factor_of = factor_of * jnp.repeat(steps, shape[axis_at] // shards_of).reshape([-1 if axis == axis_at else 1 for axis in range(len(shape))])
    return factor_of


def rank_bounds(count, lean):
    portions = [(1 << 20) // math.isqrt(standing ** lean) + 1 for standing in range(1, count + 1)]
    width = 1 + sum(portions) // (1 << 30)
    return np.cumsum(np.array([max(1, weight // width) for weight in portions]))


def ranked_ids(own_key, dims, count, lean):
    listing = rank_bounds(count, lean)
    pick = jax.random.randint(jax.random.fold_in(own_key, 1), dims, 0, int(listing[count - 1]))
    standing = jnp.searchsorted(jnp.asarray(listing, jnp.int32), pick, side="right")
    return jax.random.permutation(jax.random.fold_in(own_key, 2), count)[standing].astype(jnp.int32)


def gaussian(own_key, shape, spread, reach, cuts=(), held_as=jnp.bfloat16):
    drawn = spread * jax.random.normal(own_key, shape, jnp.float32)
    if cuts:
        drawn = drawn * shard_levels(own_key, shape, cuts, -0.22, 0.18)
    return jnp.clip(drawn, -reach, reach).astype(held_as)


def setup_inputs(seed: int = 0) -> dict:
    keys = jax.random.split(jax.random.key(seed), 10)
    return {
        "item_ids": touch_ends(ranked_ids(keys[0], (EVENTS,), VOCAB, 2), jax.random.fold_in(keys[0], 3), 0, VOCAB - 1).astype(jnp.int32),
        "domains": draw_domains(jax.random.fold_in(keys[9], 71), 0),
        "live_counts": draw_live_counts(jax.random.fold_in(keys[9], 71), 0),
        "table": draw_table(jax.random.fold_in(keys[9], 71), 0),
        "norm_gains": jnp.clip(1.0 + 0.15 * jax.random.normal(keys[4], (3, D), jnp.float32), 0.25, 1.75),
        "proj_in": gaussian(keys[5], (D, 4 * D), D ** -0.5, 0.25),
        "proj_out": gaussian(keys[6], (D, D), D ** -0.5, 0.25),
        "expert_in": gaussian(keys[7], (EXPERTS, D, 2 * HID), D ** -0.5, 0.25, ((0, 4),)),
        "expert_out": gaussian(keys[8], (EXPERTS, HID, D), HID ** -0.5, 0.125, ((0, 4),)),
    }


norm_eps = 1e-06

def rms_norm(values, gain):
    return values * lax.rsqrt(lax.optimization_barrier(jnp.mean(values * values, axis=-1, keepdims=True)) + norm_eps) * gain

def reference(item_ids, domains, live_counts, table, norm_gains, proj_in, proj_out, expert_in, expert_out):
    embedded = table[item_ids].astype(jnp.float32)
    positions = jnp.arange(ROWS, dtype=jnp.int32)
    live_mask = (positions[None, :] < live_counts[:, None]).astype(jnp.float32).reshape(EVENTS)
    normed = (rms_norm(embedded, norm_gains[0]) * live_mask[:, None]).astype(jnp.bfloat16)
    projected = jnp.dot(normed, proj_in, preferred_element_type=jnp.float32)
    gating = jax.nn.silu(projected[:, :D])
    queries, key_rows, values = lax.optimization_barrier((projected[:, D:2 * D].astype(jnp.bfloat16), projected[:, 2 * D:3 * D].astype(jnp.bfloat16), projected[:, 3 * D:].astype(jnp.bfloat16)))
    margin = SPAN * ROWS
    window = (2 * SPAN + 1) * ROWS
    key_pad = jnp.pad(key_rows, ((margin, margin), (0, 0)))
    value_pad = jnp.pad(values, ((margin, margin), (0, 0)))
    score_scale = 1.0 / math.sqrt(HEAD_DIM)
    offsets = jnp.arange(ROWS, dtype=jnp.int32)[:, None] + margin - jnp.arange(window, dtype=jnp.int32)[None, :]
    band_mask = (jnp.abs(offsets) <= margin).astype(jnp.float32)

    def one_block(block):
        start = (block * ROWS).astype(jnp.int32)
        query_blk = lax.dynamic_slice_in_dim(queries, start, ROWS, 0).astype(jnp.float32).reshape(ROWS, HEADS, HEAD_DIM)
        key_blk = lax.dynamic_slice_in_dim(key_pad, start, window, 0).astype(jnp.float32).reshape(window, HEADS, HEAD_DIM)
        value_blk = lax.dynamic_slice_in_dim(value_pad, start, window, 0).astype(jnp.float32).reshape(window, HEADS, HEAD_DIM)
        scores = jnp.einsum('qhd,khd->hqk', query_blk, key_blk) * score_scale
        weights = lax.optimization_barrier((jax.nn.silu(scores) * band_mask[None]).astype(jnp.bfloat16))
        return jnp.einsum('hqk,khd->qhd', weights.astype(jnp.float32), value_blk).reshape(ROWS, D)
    attended = lax.map(one_block, jnp.arange(EVENTS // ROWS, dtype=jnp.int32)).reshape(EVENTS, D)
    gated = (rms_norm(attended, norm_gains[1]) * gating).astype(jnp.bfloat16)
    hidden = embedded + jnp.dot(gated, proj_out, preferred_element_type=jnp.float32)
    routed = rms_norm(hidden, norm_gains[2]).astype(jnp.bfloat16)
    bound = CAP * (EVENTS // ROWS)

    def add_expert(expert, total):
        matches = domains == expert
        members = jnp.nonzero(matches, size=bound, fill_value=0)[0].astype(jnp.int32)
        filled = (jnp.arange(bound, dtype=jnp.int32) < jnp.sum(matches.astype(jnp.int32))).astype(jnp.float32)
        chosen = routed[members]
        gate_up = jnp.dot(chosen, expert_in[expert], preferred_element_type=jnp.float32)
        activated = (jax.nn.silu(gate_up[:, :HID]) * gate_up[:, HID:]).astype(jnp.bfloat16)
        produced = lax.optimization_barrier(jnp.dot(activated, expert_out[expert], preferred_element_type=jnp.float32).astype(jnp.bfloat16))
        return total.at[members].add(produced.astype(jnp.float32) * filled[:, None])
    expert_rows = lax.fori_loop(0, EXPERTS, add_expert, jnp.zeros((EVENTS, D), jnp.float32))
    return (live_mask[:, None] * (hidden + expert_rows)).astype(jnp.bfloat16)
```

```python
import functools
import math

import jax
import jax.numpy as jnp
from jax import lax
from jax.experimental import pallas as pl
from jax.experimental.pallas import tpu as pltpu
from jax.sharding import PartitionSpec as P

HEADS = 8
HEAD_DIM = 64
SPAN = 4
NORM_EPS = 1e-06
CHUNKS = 4
KEY_TILE = 256

F32 = jnp.float32
BF16 = jnp.bfloat16


def shifted(value, axis, steps):
    count = lax.axis_size(axis)
    first, last = (max(0, -steps), min(count, count - steps))
    return lax.ppermute(value, axis, [(source, source + steps) for source in range(first, last)])


def rotated(value, axis, steps):
    count = lax.axis_size(axis)
    return lax.ppermute(value, axis, [(source, (source + steps) % count) for source in range(count)])


def rms_norm(values, gain):
    return values * lax.rsqrt(jnp.mean(values * values, axis=-1, keepdims=True) + NORM_EPS) * gain


def half_silu(half):
    return half + half * jnp.tanh(half)


VMEM_SPEC = pl.BlockSpec(memory_space=pltpu.VMEM)
SMEM_SPEC = pl.BlockSpec(memory_space=pltpu.SMEM)


def cost(flops, nbytes):
    return pl.CostEstimate(flops=int(flops), bytes_accessed=int(nbytes), transcendentals=0)


def make_project(group, rows, block_rows, first_block, width, model_width):
    lane = model_width // group

    def kernel(scal, *refs):
        pieces = refs[:group]
        gain, weights = refs[group], refs[group + 1]
        q_ref, kv_ref, emb_ref = refs[group + 2 :]
        me = scal[0]
        offsets = (0, group - 1, 1, 2)
        for piece, offset in zip(pieces, offsets):
            column = lax.rem(me + offset, group)
            emb_ref[:, pl.ds(pl.multiple_of(column * lane, lane), lane)] = piece[...]
        for part in range(rows // block_rows):
            here = pl.ds(part * block_rows, block_rows)
            live = scal[1 + first_block + part]
            position = lax.broadcasted_iota(jnp.int32, (block_rows, 1), 0)
            mask = (position < live).astype(F32)
            embedded = emb_ref[here, :].astype(F32)
            normed = (rms_norm(embedded, gain[...]) * mask).astype(BF16)
            projected = jnp.dot(normed, weights[...], preferred_element_type=F32)
            scale = 0.5 / math.sqrt(HEAD_DIM)
            q_ref[here, :] = (projected[:, : 2 * width].astype(BF16).astype(F32) * scale).astype(
                BF16
            )
            kv_ref[here, :] = projected[:, 2 * width :].astype(BF16)

    return pl.pallas_call(
        kernel,
        out_shape=(
            jax.ShapeDtypeStruct((rows, 2 * width), BF16),
            jax.ShapeDtypeStruct((rows, 2 * width), BF16),
            jax.ShapeDtypeStruct((rows, model_width), BF16),
        ),
        in_specs=[SMEM_SPEC] + [VMEM_SPEC] * (group + 2),
        out_specs=(VMEM_SPEC,) * 3,
        cost_estimate=cost(2 * rows * model_width * 4 * width, 4 * rows * model_width),
        name="project",
    )


def pair(q_ref, q_at, kv_ref, k_at, acc_ref, acc_at, mask, live, block_rows, width):
    tiles = lax.div(live + (KEY_TILE - 1), KEY_TILE)
    rows = pl.ds(q_at, block_rows)

    def step(tile, carry):
        at = pl.ds(pl.multiple_of(k_at + tile * KEY_TILE, KEY_TILE), KEY_TILE)
        keys = kv_ref[at, :width]
        values = kv_ref[at, width:]
        low = lax.broadcasted_iota(jnp.int32, values.shape, 1) < HEAD_DIM
        zero = jnp.zeros_like(values)
        total = None
        for head in range(2):
            queries = q_ref[rows, head * width : (head + 1) * width]
            half = lax.dot_general(
                queries, keys, (((1,), (1,)), ((), ())), preferred_element_type=F32
            )
            weights = half_silu(half)
            if mask is not None:
                query_pos = lax.broadcasted_iota(jnp.int32, weights.shape, 0)
                key_pos = lax.broadcasted_iota(jnp.int32, weights.shape, 1) + tile * KEY_TILE
                keep = (
                    key_pos >= query_pos + mask[1]
                    if mask[0] == "before"
                    else key_pos <= query_pos + mask[1]
                )
                weights = jnp.where(keep, weights, 0.0)
            held = jnp.where(low, values, zero) if head == 0 else jnp.where(low, zero, values)
            term = jnp.dot(weights.astype(BF16), held, preferred_element_type=F32)
            total = term if total is None else total + term
        acc_ref[pl.ds(acc_at, block_rows), :] += total
        return carry

    lax.fori_loop(0, tiles, step, 0)


def make_attend(chunk, count, per, block_rows, width, has_neighbours):
    rows = per * block_rows
    olds = chunk

    def kernel(scal, *refs):
        refs = list(refs)
        take = lambda number: [refs.pop(0) for _ in range(number)]
        queries = take(chunk + 1)
        own = take(chunk + 1)
        before = take(1) if has_neighbours else []
        after = take(chunk) if has_neighbours else []
        old = take(olds)
        out = take(chunk + 1)
        for ref, prior in zip(out, old):
            ref[...] = prior[...]
        out[chunk][...] = jnp.zeros_like(out[chunk])
        blocks = count * per

        def run(q, kv_ref, k, mask, live_index):
            pair(
                queries[q // per],
                (q % per) * block_rows,
                kv_ref,
                (k % per) * block_rows,
                out[q // per],
                (q % per) * block_rows,
                mask,
                scal[1 + live_index],
                block_rows,
                width,
            )

        fresh = range(chunk * per, (chunk + 1) * per)
        known = range((chunk + 1) * per)
        for q in known:
            for k in known:
                if q in fresh or k in fresh:
                    run(q, own[k // per], k, None, k)
        if has_neighbours:
            came = range((chunk - 1) * per, chunk * per)
            for k in came:
                for q in range(k + 1):
                    run(q, before[0], k, ("before", 0) if q == k else None, blocks + k)
            for k in range(chunk * per):
                for q in range(k, (chunk + 1) * per):
                    if q < chunk * per and not (k in came):
                        continue
                    run(
                        q,
                        after[k // per],
                        k,
                        ("after", 0) if q == k else None,
                        2 * blocks + k,
                    )

    inputs = 2 * (chunk + 1) + (1 + chunk if has_neighbours else 0)
    pairs = (chunk + 1) ** 2 - chunk**2 + (3 * chunk if has_neighbours else 0)
    shape = jax.ShapeDtypeStruct((rows, width), F32)
    return pl.pallas_call(
        kernel,
        out_shape=(shape,) * (chunk + 1),
        in_specs=[SMEM_SPEC] + [VMEM_SPEC] * (inputs + olds),
        out_specs=(VMEM_SPEC,) * (chunk + 1),
        input_output_aliases={1 + inputs + i: i for i in range(olds)},
        cost_estimate=cost(pairs * rows * rows * 2 * 2 * 256 * 2, (chunk + 1) * rows * width * 16),
        name=f"attend{chunk}",
    )


def make_finish(count, per, block_rows, width):
    rows = per * block_rows
    blocks = count * per
    last = count - 1

    def kernel(scal, *refs):
        refs = list(refs)
        take = lambda number: [refs.pop(0) for _ in range(number)]
        queries = take(count)
        before, after = take(2)
        old = take(count)
        out = take(blocks)
        q_scr, acc = take(2)
        me = scal[0]
        for c in range(count):
            q_scr[pl.ds(c * rows, rows), :] = queries[c][...]
            acc[pl.ds(c * rows, rows), :] = old[c][...]
        for turn in range(blocks):
            q = lax.rem(me + 1 + turn, blocks)
            at = pl.multiple_of(q * block_rows, block_rows)
            for k in range(last * per, blocks):
                live = jnp.where(q <= k, scal[1 + blocks + k], 0)
                pair(
                    q_scr,
                    at,
                    before,
                    (k % per) * block_rows,
                    acc,
                    at,
                    ("before", (q - k) * block_rows),
                    live,
                    block_rows,
                    width,
                )
                live = jnp.where(q >= k, scal[1 + 2 * blocks + k], 0)
                pair(
                    q_scr,
                    at,
                    after,
                    (k % per) * block_rows,
                    acc,
                    at,
                    ("after", (q - k) * block_rows),
                    live,
                    block_rows,
                    width,
                )
            out[turn][...] = acc[pl.ds(at, block_rows), :].astype(BF16)

    shape = jax.ShapeDtypeStruct((block_rows, width), BF16)
    return pl.pallas_call(
        kernel,
        out_shape=(shape,) * blocks,
        in_specs=[SMEM_SPEC] + [VMEM_SPEC] * (2 * count + 2),
        out_specs=(VMEM_SPEC,) * blocks,
        scratch_shapes=[
            pltpu.VMEM((blocks * block_rows, 2 * width), BF16),
            pltpu.VMEM((blocks * block_rows, width), F32),
        ],
        cost_estimate=cost(5 * block_rows**2 * 2 * 2 * 256 * 2, count * rows * width * 8),
        name="finish",
    )


def gate_kernel(scal, emb, gains, weights, out):
    rows = emb.shape[0]
    position = lax.broadcasted_iota(jnp.int32, (rows, 1), 0)
    mask = (position < scal[0]).astype(F32)
    normed = (rms_norm(emb[...].astype(F32), gains[0:1, :]) * mask).astype(BF16)
    gate = jnp.dot(normed, weights[...], preferred_element_type=F32)
    out[...] = half_silu(gate * 0.5)


def make_route(group, rows, width, model_width, capacity):
    def kernel(scal, *refs):
        pieces = refs[:group]
        gating, emb, gains, proj_out, slot = refs[group : group + 5]
        hidden_ref = refs[group + 5]
        sent = refs[group + 6 : group + 6 + group]
        att = refs[group + 6 + group]
        me = scal[0]
        for turn, piece in enumerate(pieces):
            column = lax.rem(me + group - 1 - turn, group)
            att[:, pl.ds(pl.multiple_of(column * width, width), width)] = piece[...].astype(F32)
        gated = (rms_norm(att[...], gains[1:2, :]) * gating[...]).astype(BF16)
        hidden = emb[...].astype(F32) + jnp.dot(
            gated, proj_out[...], preferred_element_type=F32
        )
        hidden_ref[...] = hidden
        routed = rms_norm(hidden, gains[2:3, :]).astype(BF16)
        for turn in range(group):
            place = lax.broadcasted_iota(jnp.int32, (capacity, rows), 0) + turn * capacity
            pick = jnp.where(place == slot[...], 1.0, 0.0).astype(BF16)
            sent[turn][...] = jnp.dot(pick, routed, preferred_element_type=F32).astype(BF16)

    return pl.pallas_call(
        kernel,
        out_shape=(jax.ShapeDtypeStruct((rows, model_width), F32),)
        + (jax.ShapeDtypeStruct((capacity, model_width), BF16),) * group,
        in_specs=[SMEM_SPEC] + [VMEM_SPEC] * (group + 5),
        out_specs=(VMEM_SPEC,) * (group + 1),
        scratch_shapes=[pltpu.VMEM((rows, model_width), F32)],
        cost_estimate=cost(6 * rows * model_width**2, 8 * rows * model_width),
        name="route",
    )


def expert_kernel(x, w_gate, w_up, w_down, out, acc):
    step = pl.program_id(0)
    gate = jnp.dot(x[...], w_gate[...], preferred_element_type=F32)
    up = jnp.dot(x[...], w_up[...], preferred_element_type=F32)
    activated = (half_silu(gate * 0.5) * up).astype(BF16)
    term = jnp.dot(activated, w_down[...], preferred_element_type=F32)

    @pl.when(step == 0)
    def _():
        acc[...] = term

    @pl.when(step > 0)
    def _():
        acc[...] += term

    @pl.when(step == pl.num_programs(0) - 1)
    def _():
        out[...] = acc[...].astype(BF16)


def make_expert(rows, model_width, hidden):
    tile = hidden // 4
    steps = hidden // tile
    return pl.pallas_call(
        expert_kernel,
        grid=(steps,),
        out_shape=jax.ShapeDtypeStruct((rows, model_width), BF16),
        in_specs=[
            pl.BlockSpec((rows, model_width), lambda i: (0, 0)),
            pl.BlockSpec((model_width, tile), lambda i: (0, i)),
            pl.BlockSpec((model_width, tile), lambda i: (0, steps + i)),
            pl.BlockSpec((tile, model_width), lambda i: (i, 0)),
        ],
        out_specs=pl.BlockSpec((rows, model_width), lambda i: (0, 0)),
        scratch_shapes=[pltpu.VMEM((rows, model_width), F32)],
        cost_estimate=cost(
            6 * rows * model_width * hidden, 6 * model_width * hidden + 4 * rows * model_width
        ),
        name="expert",
    )


def make_mix(group, rows, model_width, capacity):
    def kernel(scal, *refs):
        pieces = refs[:group]
        hidden, slot, out = refs[group:]
        total = hidden[...]
        for turn, piece in enumerate(pieces):
            place = lax.broadcasted_iota(jnp.int32, (rows, capacity), 1) + turn * capacity
            pick = jnp.where(place == slot[...], 1.0, 0.0).astype(BF16)
            total = total + jnp.dot(pick, piece[...], preferred_element_type=F32)
        position = lax.broadcasted_iota(jnp.int32, (rows, 1), 0)
        mask = (position < scal[0]).astype(F32)
        out[...] = (mask * total).astype(BF16)

    return pl.pallas_call(
        kernel,
        out_shape=jax.ShapeDtypeStruct((rows, model_width), BF16),
        in_specs=[SMEM_SPEC] + [VMEM_SPEC] * (group + 2),
        out_specs=VMEM_SPEC,
        cost_estimate=cost(2 * rows * rows * model_width * 2, 8 * rows * model_width),
        name="mix",
    )


def by_heads(
    item_ids, domains, live_counts, table, norm_gains, proj_in, proj_out, expert_in, expert_out
):
    group = lax.axis_size("emb")
    me = lax.axis_index("emb").astype(jnp.int32)
    rows = domains.shape[0]
    model_width = proj_out.shape[0]
    hidden_units = expert_out.shape[1]
    width = model_width // group
    capacity = 2 * rows // group
    per = group // CHUNKS
    chunk_rows = per * rows

    parts = []
    for c in range(CHUNKS):
        ids = item_ids[c * chunk_rows : (c + 1) * chunk_rows]
        mine = table[ids]
        low = rotated(mine, "emb", 1)
        high = rotated(mine, "emb", -1)
        far = rotated(low, "emb", 1)
        parts.append((mine, low, high, far))

    around = [live_counts] + [rotated(live_counts, "emb", -k) for k in range(1, group)]
    lives = jnp.roll(jnp.concatenate(around), me)
    lives_before = shifted(lives, "seq", 1)
    lives_after = shifted(lives, "seq", -1)
    scal = jnp.concatenate((me[None], lives, lives_before, lives_after))

    columns = lambda index: lax.dynamic_slice(
        proj_in, (0, index * model_width + me * width), (model_width, width)
    )
    w_q = columns(1)
    head = (jnp.arange(width, dtype=jnp.int32) < HEAD_DIM)[None]
    zero = jnp.zeros_like(w_q)
    weights = jnp.concatenate(
        (jnp.where(head, w_q, zero), jnp.where(head, zero, w_q), columns(2), columns(3)), axis=1
    )

    queries, own, before, after, embedded = [], [], [], [], []
    accs = []
    for c in range(CHUNKS):
        project = make_project(group, chunk_rows, rows, c * per, width, model_width)
        q, kv, emb = project(scal, *parts[c], norm_gains[0:1], weights)
        queries.append(q)
        own.append(kv)
        embedded.append(emb)
        before.append(shifted(kv, "seq", 1))
        after.append(shifted(kv, "seq", -1))
        attend = make_attend(c, CHUNKS, per, rows, width, c > 0)
        near = (before[c - 1], *after[:c]) if c > 0 else ()
        accs = list(attend(scal, *queries, *own, *near, *accs))

    finish = make_finish(CHUNKS, per, rows, width)
    heads = finish(scal, *queries, before[-1], after[-1], *accs)
    pieces = [
        heads[t] if t == group - 1 else rotated(heads[t], "emb", t + 1) for t in range(group)
    ]

    own_embedded = lax.dynamic_index_in_dim(
        jnp.concatenate(embedded).reshape(group, rows, model_width), me, 0, keepdims=False
    )
    gating = pl.pallas_call(
        gate_kernel,
        out_shape=jax.ShapeDtypeStruct((rows, model_width), F32),
        in_specs=[SMEM_SPEC] + [VMEM_SPEC] * 3,
        out_specs=VMEM_SPEC,
        cost_estimate=cost(2 * rows * model_width**2, 8 * rows * model_width),
        name="gate",
    )(live_counts, own_embedded, norm_gains, proj_in[:, :model_width])

    live_mask = jnp.arange(rows, dtype=jnp.int32) < live_counts[0]
    turn = jnp.mod(domains - me, group)
    onehot = (
        (turn[:, None] == jnp.arange(group, dtype=jnp.int32)[None, :]) & live_mask[:, None]
    ).astype(jnp.int32)
    rank = jnp.sum((jnp.cumsum(onehot, axis=0) - onehot) * onehot, axis=1)
    slot = jnp.where(live_mask, turn * capacity + rank, -1)

    route = make_route(group, rows, width, model_width, capacity)
    hidden, *sent = route(
        me[None], *pieces, gating, own_embedded, norm_gains, proj_out, slot[None, :]
    )
    expert = make_expert(capacity, model_width, hidden_units)
    arrived = [sent[0]] + [rotated(sent[k], "emb", k) for k in range(1, group)]
    returned = []
    for k in range(group):
        made = expert(arrived[k], expert_in[0], expert_in[0], expert_out[0])
        returned.append(made if k == 0 else rotated(made, "emb", -k))
    mix = make_mix(group, rows, model_width, capacity)
    return mix(live_counts, *returned, hidden, slot[:, None])


def by_rows(
    item_ids, domains, live_counts, table, norm_gains, proj_in, proj_out, expert_in, expert_out
):
    rows_dev = domains.shape[0]
    model_width = proj_out.shape[0]
    hidden_units = expert_out.shape[1]
    group_size = lax.axis_size("emb")
    capacity = 2 * rows_dev // group_size
    columns = table[item_ids]
    embedded = lax.all_to_all(columns, "emb", split_axis=0, concat_axis=1, tiled=True).astype(
        jnp.float32
    )
    positions = jnp.arange(rows_dev, dtype=jnp.int32)
    live_mask = (positions < live_counts[0]).astype(jnp.float32)
    normed = (rms_norm(embedded, norm_gains[0]) * live_mask[:, None]).astype(jnp.bfloat16)
    projected = jnp.dot(normed, proj_in, preferred_element_type=jnp.float32)
    gating = jax.nn.silu(projected[:, :model_width])
    queries = (
        projected[:, model_width : 2 * model_width]
        .astype(jnp.bfloat16)
        .reshape(rows_dev, HEADS, HEAD_DIM)
    )
    own_pair = jnp.stack(
        (
            projected[:, 2 * model_width : 3 * model_width].astype(jnp.bfloat16),
            projected[:, 3 * model_width :].astype(jnp.bfloat16),
        )
    )
    key_weights = proj_in[:, 2 * model_width :]
    upper_band = positions[None, :] >= positions[:, None]
    lower_band = positions[None, :] <= positions[:, None]
    score_scale = 1.0 / math.sqrt(HEAD_DIM)

    def unpack(piece):
        rebuilt = jnp.dot(piece[0], key_weights, preferred_element_type=jnp.float32)
        return jnp.stack(
            (
                rebuilt[:, :model_width].astype(jnp.bfloat16),
                rebuilt[:, model_width:].astype(jnp.bfloat16),
            )
        )

    def attend(both, band_mask):
        key_heads = both[0].reshape(rows_dev, HEADS, HEAD_DIM)
        value_heads = both[1].reshape(rows_dev, HEADS, HEAD_DIM)
        scores = (
            jnp.einsum("qhd,khd->hqk", queries, key_heads, preferred_element_type=jnp.float32)
            * score_scale
        )
        weights = jax.nn.silu(scores)
        if band_mask is not None:
            weights = jnp.where(band_mask[None], weights, 0.0)
        weights = weights.astype(jnp.bfloat16)
        return jnp.einsum(
            "hqk,khd->qhd", weights, value_heads, preferred_element_type=jnp.float32
        ).reshape(rows_dev, model_width)

    outgoing = normed[None]
    attended = attend(own_pair, None)
    for distance in range(1, SPAN + 1):
        band_before = upper_band if distance == SPAN else None
        band_after = lower_band if distance == SPAN else None
        earlier = shifted(outgoing, ("seq", "emb"), distance)
        following = shifted(outgoing, ("seq", "emb"), -distance)
        attended = (
            attended + attend(unpack(earlier), band_before) + attend(unpack(following), band_after)
        )
    gated = (rms_norm(attended, norm_gains[1]) * gating).astype(jnp.bfloat16)
    hidden = embedded + jnp.dot(gated, proj_out, preferred_element_type=jnp.float32)
    routed = rms_norm(hidden, norm_gains[2]).astype(jnp.bfloat16)
    onehot_domain = (domains[:, None] == jnp.arange(group_size, dtype=jnp.int32)[None, :]).astype(
        jnp.int32
    )
    slot_rank = jnp.sum((jnp.cumsum(onehot_domain, axis=0) - onehot_domain) * onehot_domain, axis=1)
    slot_index = domains * capacity + slot_rank
    outgoing_rows = (
        jnp.zeros((group_size * capacity, model_width), jnp.bfloat16).at[slot_index].set(routed)
    )
    outgoing_rows = outgoing_rows.reshape(group_size, capacity, model_width)
    inbox = lax.all_to_all(outgoing_rows, "emb", split_axis=0, concat_axis=0, tiled=True)
    sources, slot_count, _ = inbox.shape
    flattened = inbox.reshape(sources * slot_count, model_width)
    gate_up = jnp.dot(flattened, expert_in[0], preferred_element_type=jnp.float32)
    activated = (jax.nn.silu(gate_up[:, :hidden_units]) * gate_up[:, hidden_units:]).astype(
        jnp.bfloat16
    )
    produced = jnp.dot(activated, expert_out[0], preferred_element_type=jnp.float32).astype(
        jnp.bfloat16
    )
    finished = produced.reshape(sources, slot_count, model_width)
    returned = lax.all_to_all(finished, "emb", split_axis=0, concat_axis=0, tiled=True).reshape(
        group_size * capacity, model_width
    )
    expert_rows = returned[slot_index].astype(jnp.float32)
    return (live_mask[:, None] * (hidden + expert_rows)).astype(jnp.bfloat16)


def solution(mesh):
    group = mesh.shape["emb"]
    body = by_heads if group == SPAN and HEADS == 2 * group else by_rows
    in_specs = (
        P("seq"),
        P(("seq", "emb")),
        P(("seq", "emb")),
        P(None, "emb"),
        P(),
        P(),
        P(),
        P("emb", None, None),
        P("emb", None, None),
    )
    out_specs = P(("seq", "emb"), None)
    return jax.shard_map(body, mesh=mesh, in_specs=in_specs, out_specs=out_specs, check_vma=False)
```

```python
import functools
import math

import jax
import jax.numpy as jnp
from jax import lax
from jax.experimental import pallas as pl
from jax.experimental.pallas import tpu as pltpu
from jax.sharding import PartitionSpec as P

HEADS = 8
HEAD_DIM = 64
SPAN = 4
NORM_EPS = 1e-06
CHUNKS = 2
KEY_TILE = 256
TAIL = 16
MIB = 1 << 20

F32 = jnp.float32
BF16 = jnp.bfloat16
I32 = jnp.int32


def shifted(value, axis, steps):
    count = lax.axis_size(axis)
    first, last = (max(0, -steps), min(count, count - steps))
    return lax.ppermute(value, axis, [(source, source + steps) for source in range(first, last)])


def rotated(value, axis, steps):
    count = lax.axis_size(axis)
    return lax.ppermute(value, axis, [(source, (source + steps) % count) for source in range(count)])


def rms_norm(values, gain):
    return values * lax.rsqrt(jnp.mean(values * values, axis=-1, keepdims=True) + NORM_EPS) * gain


def half_silu(half):
    return half + half * jnp.tanh(half)


VMEM_SPEC = pl.BlockSpec(memory_space=pltpu.VMEM)
SMEM_SPEC = pl.BlockSpec(memory_space=pltpu.SMEM)


def cost(flops, nbytes):
    return pl.CostEstimate(flops=int(flops), bytes_accessed=int(nbytes), transcendentals=0)


def limit(mib):
    return pltpu.CompilerParams(vmem_limit_bytes=mib * MIB)


def make_weights(model_width, width):
    def kernel(me, w_q, w_k, w_v, out):
        queries = w_q[...]
        low = lax.broadcasted_iota(I32, queries.shape, 1) < HEAD_DIM
        zero = jnp.zeros_like(queries)
        out[:, :width] = jnp.where(low, queries, zero)
        out[:, width : 2 * width] = jnp.where(low, zero, queries)
        out[:, 2 * width : 3 * width] = w_k[...]
        out[:, 3 * width :] = w_v[...]

    per = model_width // width
    block = lambda index: pl.BlockSpec(
        (model_width, width), lambda i, me: (0, index * per + me[0])
    )
    return pl.pallas_call(
        kernel,
        grid_spec=pltpu.PrefetchScalarGridSpec(
            num_scalar_prefetch=1,
            grid=(1,),
            in_specs=[block(1), block(2), block(3)],
            out_specs=pl.BlockSpec((model_width, 4 * width), lambda i, me: (0, 0)),
        ),
        out_shape=jax.ShapeDtypeStruct((model_width, 4 * width), BF16),
        compiler_params=limit(4),
        cost_estimate=cost(0, 16 * model_width * width),
        name="weights",
    )


def make_project(group, chunk, rows, block_rows, width, model_width):
    lane = model_width // group
    per = rows // block_rows
    opening = chunk == 0

    def kernel(me_ref, *refs):
        refs = list(refs)
        take = lambda number: [refs.pop(0) for _ in range(number)]
        known = None if opening else take(1)[0]
        pieces = take(group)
        gains, weights = take(2)
        q_ref, kv_ref, own_ref = take(3)
        lives_ref = take(1)[0] if opening else None
        emb_ref = take(1)[0]
        me = me_ref[0]
        offsets = (0, group - 1, 1, 2)
        for piece, offset in zip(pieces, offsets):
            column = lax.rem(me + offset, group)
            emb_ref[:, pl.ds(pl.multiple_of(column * lane, lane), lane)] = piece[:rows, :]
            if opening:
                code = piece[rows : rows + TAIL, :].astype(F32)
                high, low = jnp.max(code[: TAIL // 2]), jnp.max(code[TAIL // 2 :])
                lives_ref[column] = (high * TAIL + low).astype(I32)
        lives = [(lives_ref if opening else known)[b] for b in range(group)]
        for part in range(per):
            here = pl.ds(part * block_rows, block_rows)
            position = lax.broadcasted_iota(I32, (block_rows, 1), 0)
            mask = (position < lives[chunk * per + part]).astype(F32)
            embedded = emb_ref[here, :].astype(F32)
            normed = (rms_norm(embedded, gains[0:1, :]) * mask).astype(BF16)
            projected = jnp.dot(normed, weights[...], preferred_element_type=F32)
            scale = 0.5 / math.sqrt(HEAD_DIM)
            q_ref[here, :] = projected[:, : 2 * width].astype(BF16) * jnp.asarray(scale, BF16)
            kv_ref[here, :] = projected[:, 2 * width :].astype(BF16)
        if opening:
            row = lax.broadcasted_iota(I32, (TAIL, 2 * width), 0)
            code = jnp.zeros((TAIL, 2 * width), F32)
            for b in range(group):
                high = lax.div(lives[b], TAIL)
                code = jnp.where(row == b, high.astype(F32), code)
                code = jnp.where(row == group + b, (lives[b] - high * TAIL).astype(F32), code)
            kv_ref[pl.ds(rows, TAIL), :] = code.astype(BF16)
        at = lax.rem(me, per) * block_rows
        own_ref[...] = emb_ref[pl.ds(pl.multiple_of(at, block_rows), block_rows), :]

    more = TAIL if opening else 0
    out_shape = (
        jax.ShapeDtypeStruct((rows, 2 * width), BF16),
        jax.ShapeDtypeStruct((rows + more, 2 * width), BF16),
        jax.ShapeDtypeStruct((block_rows, model_width), BF16),
    )
    out_specs = (VMEM_SPEC,) * 3
    if opening:
        out_shape += (jax.ShapeDtypeStruct((group,), I32),)
        out_specs += (SMEM_SPEC,)
    return pl.pallas_call(
        kernel,
        out_shape=out_shape,
        in_specs=[SMEM_SPEC] * (1 if opening else 2) + [VMEM_SPEC] * (group + 2),
        out_specs=out_specs,
        scratch_shapes=[pltpu.VMEM((rows, model_width), BF16)],
        compiler_params=limit(16),
        cost_estimate=cost(2 * rows * model_width * 4 * width, 4 * rows * model_width),
        name=f"project{chunk}",
    )


def pair(queries, q_at, q_pos, kv_ref, k_at, k_pos, acc_ref, acc_at, rows, keep, live, width):
    tiles = lax.div(live + (KEY_TILE - 1), KEY_TILE)

    def step(tile, carry):
        at = pl.ds(pl.multiple_of(k_at + tile * KEY_TILE, KEY_TILE), KEY_TILE)
        keys = kv_ref[at, :width]
        values = kv_ref[at, width:]
        low = lax.broadcasted_iota(I32, values.shape, 1) < HEAD_DIM
        zero = jnp.zeros_like(values)
        total = None
        for head in range(2):
            half = lax.dot_general(
                queries[pl.ds(q_at, rows), head * width : (head + 1) * width],
                keys,
                (((1,), (1,)), ((), ())),
                preferred_element_type=F32,
            )
            weights = half_silu(half)
            if keep is not None:
                query = lax.broadcasted_iota(I32, weights.shape, 0) + q_pos
                key = lax.broadcasted_iota(I32, weights.shape, 1) + (k_pos + tile * KEY_TILE)
                weights = jnp.where(keep(query, key), weights, 0.0)
            held = jnp.where(low, values, zero) if head == 0 else jnp.where(low, zero, values)
            term = jnp.dot(weights.astype(BF16), held, preferred_element_type=F32)
            total = term if total is None else total + term
        acc_ref[pl.ds(acc_at, rows), :] += total
        return carry

    lax.fori_loop(0, tiles, step, 0)


def from_before(query, key):
    return key >= query


def from_after(query, key):
    return key <= query


def read_lives(kv_ref, rows, group):
    code = kv_ref[pl.ds(rows, TAIL), :].astype(F32)
    return [
        (jnp.max(code[b : b + 1]) * TAIL + jnp.max(code[group + b : group + b + 1])).astype(I32)
        for b in range(group)
    ]


def make_attend(chunk, count, per, block_rows, width):
    rows = per * block_rows
    group = count * per
    beside = chunk > 0

    def kernel(lives_ref, *refs):
        refs = list(refs)
        take = lambda number: [refs.pop(0) for _ in range(number)]
        queries = take(chunk + 1)
        own = take(chunk + 1)
        before = take(chunk)
        after = take(chunk)
        old = take(chunk)
        out = take(chunk + 1)
        for ref, prior in zip(out, old):
            ref[...] = prior[...]
        out[chunk][...] = jnp.zeros_like(out[chunk])

        def run(c, first, last, kv_ref, k, keep, live):
            at = (first - c * per) * block_rows
            pair(
                queries[c],
                at,
                first * block_rows,
                kv_ref,
                (k % per) * block_rows,
                k * block_rows,
                out[c],
                at,
                (last - first) * block_rows,
                keep,
                live,
                width,
            )

        for c in range(chunk + 1):
            for k in range((chunk + 1) * per):
                if c == chunk or k // per == chunk:
                    run(c, c * per, (c + 1) * per, own[k // per], k, None, lives_ref[k])
        if beside:
            lives_before = read_lives(before[0], rows, group)
            lives_after = read_lives(after[0], rows, group)
            for k in range((chunk - 1) * per, chunk * per):
                for c in range(chunk):
                    last = min((c + 1) * per, k + 1)
                    if last > c * per:
                        run(c, c * per, last, before[k // per], k, from_before, lives_before[k])
            for k in range(chunk * per):
                for c in range(chunk + 1):
                    if c < chunk and k // per < chunk - 1:
                        continue
                    first = max(c * per, k)
                    if first < (c + 1) * per:
                        run(c, first, (c + 1) * per, after[k // per], k, from_after, lives_after[k])

    inputs = 2 * (chunk + 1) + 2 * chunk
    pairs = per * per * ((chunk + 1) ** 2 - chunk**2 + 2 * chunk)
    shape = jax.ShapeDtypeStruct((rows, width), F32)
    return pl.pallas_call(
        kernel,
        out_shape=(shape,) * (chunk + 1),
        in_specs=[SMEM_SPEC] + [VMEM_SPEC] * (inputs + chunk),
        out_specs=(VMEM_SPEC,) * (chunk + 1),
        compiler_params=limit(28),
        cost_estimate=cost(pairs * block_rows**2 * 2048, (chunk + 1) * rows * width * 16),
        name=f"attend{chunk}",
    )


def make_finish(count, per, block_rows, width):
    rows = per * block_rows
    blocks = count * per
    last = count - 1

    def kernel(me_ref, *refs):
        refs = list(refs)
        take = lambda number: [refs.pop(0) for _ in range(number)]
        queries = take(count)
        before, after = take(2)
        first_before, first_after = take(2)
        old = take(count)
        out = take(blocks)
        q_scr, acc = take(2)
        me = me_ref[0]
        lives_before = read_lives(first_before, rows, blocks)
        lives_after = read_lives(first_after, rows, blocks)
        for c in range(count):
            q_scr[pl.ds(c * rows, rows), :] = queries[c][...]
            acc[pl.ds(c * rows, rows), :] = old[c][...]
        for turn in range(blocks):
            q = lax.rem(me + 1 + turn, blocks)
            at = pl.multiple_of(q * block_rows, block_rows)
            for k in range(last * per, blocks):
                for kv_ref, keep, live in (
                    (before, from_before, jnp.where(q <= k, lives_before[k], 0)),
                    (after, from_after, jnp.where(q >= k, lives_after[k], 0)),
                ):
                    pair(
                        q_scr,
                        at,
                        at,
                        kv_ref,
                        (k % per) * block_rows,
                        k * block_rows,
                        acc,
                        at,
                        block_rows,
                        keep,
                        live,
                        width,
                    )
            out[turn][...] = acc[pl.ds(at, block_rows), :].astype(BF16)

    shape = jax.ShapeDtypeStruct((block_rows, width), BF16)
    return pl.pallas_call(
        kernel,
        out_shape=(shape,) * blocks,
        in_specs=[SMEM_SPEC] + [VMEM_SPEC] * (2 * count + 4),
        out_specs=(VMEM_SPEC,) * blocks,
        scratch_shapes=[
            pltpu.VMEM((blocks * block_rows, 2 * width), BF16),
            pltpu.VMEM((blocks * block_rows, width), F32),
        ],
        compiler_params=limit(24),
        cost_estimate=cost(10 * block_rows**2 * 2048, count * rows * width * 8),
        name="finish",
    )


def make_gate(group, count, rows, model_width, capacity):
    per = group // count

    def kernel(me_ref, live_ref, *refs):
        candidates = refs[:count]
        gains, weights, domains, gating, emb_ref, slot_row, slot_col = refs[count:]
        me, live = me_ref[0], live_ref[0]
        for c in range(count):

            @pl.when(lax.div(me, per) == c)
            def _():
                emb_ref[...] = candidates[c][...]

        position = lax.broadcasted_iota(I32, (rows, 1), 0)
        mask = (position < live).astype(F32)
        normed = (rms_norm(emb_ref[...].astype(F32), gains[0:1, :]) * mask).astype(BF16)
        gate = jnp.dot(normed, weights[...], preferred_element_type=F32)
        gating[...] = half_silu(gate * 0.5)
        turn = lax.rem(domains[...] - me + group, group)
        alive = lax.broadcasted_iota(I32, (1, rows), 1) < live
        expert = lax.broadcasted_iota(I32, (8, rows), 0)
        onehot = jnp.where((expert == turn) & alive, 1.0, 0.0)
        earlier = lax.broadcasted_iota(I32, (rows, rows), 0) < lax.broadcasted_iota(
            I32, (rows, rows), 1
        )
        rank = jnp.dot(
            onehot.astype(BF16),
            jnp.where(earlier, 1.0, 0.0).astype(BF16),
            preferred_element_type=F32,
        )
        slot = jnp.sum(onehot * (rank + (expert * capacity).astype(F32)), axis=0, keepdims=True)
        slot = jnp.where(alive, slot, -1.0)
        slot_row[...] = slot.astype(I32)
        slot_col[...] = jnp.transpose(jnp.broadcast_to(slot, (128, rows))).astype(I32)

    return pl.pallas_call(
        kernel,
        grid=(1,),
        out_shape=(
            jax.ShapeDtypeStruct((rows, model_width), F32),
            jax.ShapeDtypeStruct((rows, model_width), BF16),
            jax.ShapeDtypeStruct((1, rows), I32),
            jax.ShapeDtypeStruct((rows, 128), I32),
        ),
        in_specs=[SMEM_SPEC] * 2
        + [VMEM_SPEC] * (count + 1)
        + [pl.BlockSpec((model_width, model_width), lambda i: (0, 0)), VMEM_SPEC],
        out_specs=(VMEM_SPEC,) * 4,
        compiler_params=limit(12),
        cost_estimate=cost(2 * rows * model_width**2, 8 * rows * model_width),
        name="gate",
    )


def make_route(group, rows, width, model_width, capacity):
    def kernel(me_ref, *refs):
        pieces = refs[:group]
        gating, emb, gains, proj_out, slot = refs[group : group + 5]
        hidden_ref = refs[group + 5]
        sent = refs[group + 6 : group + 6 + group]
        att = refs[group + 6 + group]
        me = me_ref[0]
        for turn, piece in enumerate(pieces):
            column = lax.rem(me + group - 1 - turn, group)
            att[:, pl.ds(pl.multiple_of(column * width, width), width)] = piece[...].astype(F32)
        gated = (rms_norm(att[...], gains[1:2, :]) * gating[...]).astype(BF16)
        hidden = emb[...].astype(F32) + jnp.dot(
            gated, proj_out[...], preferred_element_type=F32
        )
        hidden_ref[...] = hidden
        routed = rms_norm(hidden, gains[2:3, :]).astype(BF16)
        for turn in range(group):
            place = lax.broadcasted_iota(I32, (capacity, rows), 0) + turn * capacity
            pick = jnp.where(place == slot[...], 1.0, 0.0).astype(BF16)
            sent[turn][...] = jnp.dot(pick, routed, preferred_element_type=F32).astype(BF16)

    return pl.pallas_call(
        kernel,
        out_shape=(jax.ShapeDtypeStruct((rows, model_width), F32),)
        + (jax.ShapeDtypeStruct((capacity, model_width), BF16),) * group,
        in_specs=[SMEM_SPEC] + [VMEM_SPEC] * (group + 5),
        out_specs=(VMEM_SPEC,) * (group + 1),
        scratch_shapes=[pltpu.VMEM((rows, model_width), F32)],
        compiler_params=limit(16),
        cost_estimate=cost(6 * rows * model_width**2, 8 * rows * model_width),
        name="route",
    )


def make_expert(rows, model_width, hidden):
    tile = hidden // 4

    def kernel(x, w_in, w_out, out):
        total = None
        for at in range(0, hidden, tile):
            gate = jnp.dot(x[...], w_in[0, :, at : at + tile], preferred_element_type=F32)
            up = jnp.dot(
                x[...], w_in[0, :, hidden + at : hidden + at + tile], preferred_element_type=F32
            )
            activated = (half_silu(gate * 0.5) * up).astype(BF16)
            term = jnp.dot(activated, w_out[0, at : at + tile, :], preferred_element_type=F32)
            total = term if total is None else total + term
        out[...] = total.astype(BF16)

    return pl.pallas_call(
        kernel,
        out_shape=jax.ShapeDtypeStruct((rows, model_width), BF16),
        in_specs=[VMEM_SPEC] * 3,
        out_specs=VMEM_SPEC,
        compiler_params=limit(16),
        cost_estimate=cost(6 * rows * model_width * hidden, 4 * rows * model_width),
        name="expert",
    )


def make_mix(group, rows, model_width, capacity):
    def kernel(live_ref, *refs):
        pieces = refs[:group]
        hidden, slot, out = refs[group:]
        total = hidden[...]
        where = slot[:, 0:1]
        for turn, piece in enumerate(pieces):
            place = lax.broadcasted_iota(I32, (rows, capacity), 1) + turn * capacity
            pick = jnp.where(place == where, 1.0, 0.0).astype(BF16)
            total = total + jnp.dot(pick, piece[...], preferred_element_type=F32)
        position = lax.broadcasted_iota(I32, (rows, 1), 0)
        mask = (position < live_ref[0]).astype(F32)
        out[...] = (mask * total).astype(BF16)

    return pl.pallas_call(
        kernel,
        out_shape=jax.ShapeDtypeStruct((rows, model_width), BF16),
        in_specs=[SMEM_SPEC] + [VMEM_SPEC] * (group + 2),
        out_specs=VMEM_SPEC,
        compiler_params=limit(12),
        cost_estimate=cost(2 * rows * rows * model_width * 2, 8 * rows * model_width),
        name="mix",
    )


def by_heads(
    item_ids, domains, live_counts, table, norm_gains, proj_in, proj_out, expert_in, expert_out
):
    group = lax.axis_size("emb")
    me = lax.axis_index("emb").astype(I32)[None]
    rows = domains.shape[0]
    model_width = proj_out.shape[0]
    hidden_units = expert_out.shape[1]
    width = model_width // group
    capacity = 2 * rows // group
    per = group // CHUNKS
    chunk_rows = per * rows

    high = lax.div(live_counts[0], TAIL)
    code = jnp.where(jnp.arange(TAIL, dtype=I32) < TAIL // 2, high, live_counts[0] - high * TAIL)
    code = jnp.broadcast_to(code.astype(BF16)[:, None], (TAIL, width))
    parts = []
    for c in range(CHUNKS):
        mine = table[item_ids[c * chunk_rows : (c + 1) * chunk_rows]]
        if c == 0:
            mine = jnp.concatenate((mine, code))
        low = rotated(mine, "emb", 1)
        high = rotated(mine, "emb", -1)
        far = rotated(low, "emb", 1)
        parts.append((mine, low, high, far))

    weights = make_weights(model_width, width)(me, proj_in, proj_in, proj_in)
    queries, own, before, after, candidates, accs = [], [], [], [], [], []
    lives = None
    for c in range(CHUNKS):
        project = make_project(group, c, chunk_rows, rows, width, model_width)
        known = () if c == 0 else (lives,)
        q, kv, emb, *more = project(me, *known, *parts[c], norm_gains, weights)
        lives = more[0] if c == 0 else lives
        queries.append(q)
        own.append(kv)
        candidates.append(emb)
        before.append(shifted(kv, "seq", 1))
        after.append(shifted(kv, "seq", -1))
        attend = make_attend(c, CHUNKS, per, rows, width)
        accs = list(attend(lives, *queries, *own, *before[:c], *after[:c], *accs))

    gating, own_embedded, slot_row, slot_col = make_gate(
        group, CHUNKS, rows, model_width, capacity
    )(me, live_counts, *candidates, norm_gains, proj_in, domains[None, :])

    finish = make_finish(CHUNKS, per, rows, width)
    heads = finish(me, *queries, before[-1], after[-1], before[0], after[0], *accs)
    pieces = [
        heads[t] if t == group - 1 else rotated(heads[t], "emb", t + 1) for t in range(group)
    ]
    route = make_route(group, rows, width, model_width, capacity)
    hidden, *sent = route(me, *pieces, gating, own_embedded, norm_gains, proj_out, slot_row)
    expert = make_expert(capacity, model_width, hidden_units)
    arrived = [sent[0]] + [rotated(sent[k], "emb", k) for k in range(1, group)]
    returned = []
    for k in range(group):
        made = expert(arrived[k], expert_in, expert_out)
        returned.append(made if k == 0 else rotated(made, "emb", -k))
    mix = make_mix(group, rows, model_width, capacity)
    return mix(live_counts, *returned, hidden, slot_col)


def by_rows(
    item_ids, domains, live_counts, table, norm_gains, proj_in, proj_out, expert_in, expert_out
):
    rows_dev = domains.shape[0]
    model_width = proj_out.shape[0]
    hidden_units = expert_out.shape[1]
    group_size = lax.axis_size("emb")
    capacity = 2 * rows_dev // group_size
    columns = table[item_ids]
    embedded = lax.all_to_all(columns, "emb", split_axis=0, concat_axis=1, tiled=True).astype(
        jnp.float32
    )
    positions = jnp.arange(rows_dev, dtype=jnp.int32)
    live_mask = (positions < live_counts[0]).astype(jnp.float32)
    normed = (rms_norm(embedded, norm_gains[0]) * live_mask[:, None]).astype(jnp.bfloat16)
    projected = jnp.dot(normed, proj_in, preferred_element_type=jnp.float32)
    gating = jax.nn.silu(projected[:, :model_width])
    queries = (
        projected[:, model_width : 2 * model_width]
        .astype(jnp.bfloat16)
        .reshape(rows_dev, HEADS, HEAD_DIM)
    )
    own_pair = jnp.stack(
        (
            projected[:, 2 * model_width : 3 * model_width].astype(jnp.bfloat16),
            projected[:, 3 * model_width :].astype(jnp.bfloat16),
        )
    )
    key_weights = proj_in[:, 2 * model_width :]
    upper_band = positions[None, :] >= positions[:, None]
    lower_band = positions[None, :] <= positions[:, None]
    score_scale = 1.0 / math.sqrt(HEAD_DIM)

    def unpack(piece):
        rebuilt = jnp.dot(piece[0], key_weights, preferred_element_type=jnp.float32)
        return jnp.stack(
            (
                rebuilt[:, :model_width].astype(jnp.bfloat16),
                rebuilt[:, model_width:].astype(jnp.bfloat16),
            )
        )

    def attend(both, band_mask):
        key_heads = both[0].reshape(rows_dev, HEADS, HEAD_DIM)
        value_heads = both[1].reshape(rows_dev, HEADS, HEAD_DIM)
        scores = (
            jnp.einsum("qhd,khd->hqk", queries, key_heads, preferred_element_type=jnp.float32)
            * score_scale
        )
        weights = jax.nn.silu(scores)
        if band_mask is not None:
            weights = jnp.where(band_mask[None], weights, 0.0)
        weights = weights.astype(jnp.bfloat16)
        return jnp.einsum(
            "hqk,khd->qhd", weights, value_heads, preferred_element_type=jnp.float32
        ).reshape(rows_dev, model_width)

    outgoing = normed[None]
    attended = attend(own_pair, None)
    for distance in range(1, SPAN + 1):
        band_before = upper_band if distance == SPAN else None
        band_after = lower_band if distance == SPAN else None
        earlier = shifted(outgoing, ("seq", "emb"), distance)
        following = shifted(outgoing, ("seq", "emb"), -distance)
        attended = (
            attended + attend(unpack(earlier), band_before) + attend(unpack(following), band_after)
        )
    gated = (rms_norm(attended, norm_gains[1]) * gating).astype(jnp.bfloat16)
    hidden = embedded + jnp.dot(gated, proj_out, preferred_element_type=jnp.float32)
    routed = rms_norm(hidden, norm_gains[2]).astype(jnp.bfloat16)
    onehot_domain = (domains[:, None] == jnp.arange(group_size, dtype=jnp.int32)[None, :]).astype(
        jnp.int32
    )
    slot_rank = jnp.sum((jnp.cumsum(onehot_domain, axis=0) - onehot_domain) * onehot_domain, axis=1)
    slot_index = domains * capacity + slot_rank
    outgoing_rows = (
        jnp.zeros((group_size * capacity, model_width), jnp.bfloat16).at[slot_index].set(routed)
    )
    outgoing_rows = outgoing_rows.reshape(group_size, capacity, model_width)
    inbox = lax.all_to_all(outgoing_rows, "emb", split_axis=0, concat_axis=0, tiled=True)
    sources, slot_count, _ = inbox.shape
    flattened = inbox.reshape(sources * slot_count, model_width)
    gate_up = jnp.dot(flattened, expert_in[0], preferred_element_type=jnp.float32)
    activated = (jax.nn.silu(gate_up[:, :hidden_units]) * gate_up[:, hidden_units:]).astype(
        jnp.bfloat16
    )
    produced = jnp.dot(activated, expert_out[0], preferred_element_type=jnp.float32).astype(
        jnp.bfloat16
    )
    finished = produced.reshape(sources, slot_count, model_width)
    returned = lax.all_to_all(finished, "emb", split_axis=0, concat_axis=0, tiled=True).reshape(
        group_size * capacity, model_width
    )
    expert_rows = returned[slot_index].astype(jnp.float32)
    return (live_mask[:, None] * (hidden + expert_rows)).astype(jnp.bfloat16)


def solution(mesh):
    group = mesh.shape["emb"]
    body = by_heads if group == SPAN and HEADS == 2 * group else by_rows
    in_specs = (
        P("seq"),
        P(("seq", "emb")),
        P(("seq", "emb")),
        P(None, "emb"),
        P(),
        P(),
        P(),
        P("emb", None, None),
        P("emb", None, None),
    )
    out_specs = P(("seq", "emb"), None)
    return jax.shard_map(body, mesh=mesh, in_specs=in_specs, out_specs=out_specs, check_vma=False)
```

```python
import math

import jax
import jax.numpy as jnp
from jax import lax
from jax.experimental import pallas as pl
from jax.experimental.pallas import tpu as pltpu
from jax.sharding import PartitionSpec as P


HEADS = 8
HEAD_DIM = 64
SPAN = 4
NORM_EPS = 1e-06
CHUNKS = (0.5, 0.25, 0.25)
KEY_TILE = 256
TAIL = 16
MIB = 1 << 20

F32 = jnp.float32
BF16 = jnp.bfloat16
I32 = jnp.int32


def shifted(value, axis, steps):
    count = lax.axis_size(axis)
    first, last = (max(0, -steps), min(count, count - steps))
    return lax.ppermute(value, axis, [(source, source + steps) for source in range(first, last)])


def rotated(value, axis, steps):
    count = lax.axis_size(axis)
    return lax.ppermute(value, axis, [(source, (source + steps) % count) for source in range(count)])


def rms_norm(values, gain):
    return values * lax.rsqrt(jnp.mean(values * values, axis=-1, keepdims=True) + NORM_EPS) * gain


def half_silu(half):
    return half + half * jnp.tanh(half)


VMEM_SPEC = pl.BlockSpec(memory_space=pltpu.VMEM)
SMEM_SPEC = pl.BlockSpec(memory_space=pltpu.SMEM)


def cost(flops, nbytes):
    return pl.CostEstimate(flops=int(flops), bytes_accessed=int(nbytes), transcendentals=0)


def limit(mib):
    return pltpu.CompilerParams(vmem_limit_bytes=mib * MIB)


def make_weights(model_width, width):
    def kernel(me, w_q, w_k, w_v, out):
        queries = w_q[...]
        low = lax.broadcasted_iota(I32, queries.shape, 1) < HEAD_DIM
        zero = jnp.zeros_like(queries)
        out[:, :width] = jnp.where(low, queries, zero)
        out[:, width : 2 * width] = jnp.where(low, zero, queries)
        out[:, 2 * width : 3 * width] = w_k[...]
        out[:, 3 * width :] = w_v[...]

    per = model_width // width
    block = lambda index: pl.BlockSpec(
        (model_width, width), lambda i, me: (0, index * per + me[0])
    )
    return pl.pallas_call(
        kernel,
        grid_spec=pltpu.PrefetchScalarGridSpec(
            num_scalar_prefetch=1,
            grid=(1,),
            in_specs=[block(1), block(2), block(3)],
            out_specs=pl.BlockSpec((model_width, 4 * width), lambda i, me: (0, 0)),
        ),
        out_shape=jax.ShapeDtypeStruct((model_width, 4 * width), BF16),
        compiler_params=limit(4),
        cost_estimate=cost(0, 16 * model_width * width),
        name="weights",
    )


def make_project(group, blocks, block_rows, width, model_width):
    lane = model_width // group
    first, past = blocks
    per = past - first
    rows = per * block_rows
    opening = first == 0

    def kernel(me_ref, *refs):
        refs = list(refs)
        take = lambda number: [refs.pop(0) for _ in range(number)]
        known = None if opening else take(1)[0]
        pieces = take(group)
        gains, weights = take(2)
        q_ref, kv_ref, own_ref = take(3)
        lives_ref = take(1)[0] if opening else None
        emb_ref = take(1)[0]
        me = me_ref[0]
        offsets = (0, group - 1, 1, 2)
        for piece, offset in zip(pieces, offsets):
            column = lax.rem(me + offset, group)
            emb_ref[:, pl.ds(pl.multiple_of(column * lane, lane), lane)] = piece[pl.ds(0, rows), :]
            if opening:
                code = piece[rows : rows + TAIL, :].astype(F32)
                high, low = jnp.max(code[: TAIL // 2]), jnp.max(code[TAIL // 2 :])
                lives_ref[column] = (high * TAIL + low).astype(I32)
        lives = [(lives_ref if opening else known)[b] for b in range(group)]
        for part in range(per):
            here = pl.ds(part * block_rows, block_rows)
            position = lax.broadcasted_iota(I32, (block_rows, 1), 0)
            mask = (position < lives[first + part]).astype(F32)
            embedded = emb_ref[here, :].astype(F32)
            normed = (rms_norm(embedded, gains[0:1, :]) * mask).astype(BF16)
            projected = jnp.dot(normed, weights[...], preferred_element_type=F32)
            scale = 0.5 / math.sqrt(HEAD_DIM)
            q_ref[here, :] = projected[:, : 2 * width].astype(BF16) * jnp.asarray(scale, BF16)
            kv_ref[here, :] = projected[:, 2 * width :].astype(BF16)
        if opening:
            row = lax.broadcasted_iota(I32, (TAIL, 2 * width), 0)
            code = jnp.zeros((TAIL, 2 * width), F32)
            for b in range(group):
                high = lax.div(lives[b], TAIL)
                code = jnp.where(row == b, high.astype(F32), code)
                code = jnp.where(row == group + b, (lives[b] - high * TAIL).astype(F32), code)
            kv_ref[pl.ds(rows, TAIL), :] = code.astype(BF16)
        at = jnp.clip(me - first, 0, per - 1) * block_rows
        own_ref[...] = emb_ref[pl.ds(pl.multiple_of(at, block_rows), block_rows), :]

    more = TAIL if opening else 0
    out_shape = (
        jax.ShapeDtypeStruct((rows, 2 * width), BF16),
        jax.ShapeDtypeStruct((rows + more, 2 * width), BF16),
        jax.ShapeDtypeStruct((block_rows, model_width), BF16),
    )
    out_specs = (VMEM_SPEC,) * 3
    if opening:
        out_shape += (jax.ShapeDtypeStruct((group,), I32),)
        out_specs += (SMEM_SPEC,)
    return pl.pallas_call(
        kernel,
        out_shape=out_shape,
        in_specs=[SMEM_SPEC] * (1 if opening else 2) + [VMEM_SPEC] * (group + 2),
        out_specs=out_specs,
        scratch_shapes=[pltpu.VMEM((rows, model_width), BF16)],
        compiler_params=limit(16),
        cost_estimate=cost(2 * rows * model_width * 4 * width, 4 * rows * model_width),
    )


def pair(queries, q_at, q_pos, kv_ref, k_at, k_pos, acc_ref, acc_at, rows, keep, live, width):
    tiles = lax.div(live + (KEY_TILE - 1), KEY_TILE)

    def step(tile, carry):
        at = pl.ds(pl.multiple_of(k_at + tile * KEY_TILE, KEY_TILE), KEY_TILE)
        keys = kv_ref[at, :width]
        values = kv_ref[at, width:]
        low = lax.broadcasted_iota(I32, values.shape, 1) < HEAD_DIM
        zero = jnp.zeros_like(values)
        total = None
        for head in range(2):
            half = lax.dot_general(
                queries[pl.ds(q_at, rows), head * width : (head + 1) * width],
                keys,
                (((1,), (1,)), ((), ())),
                preferred_element_type=F32,
            )
            weights = half_silu(half)
            if keep is not None:
                query = lax.broadcasted_iota(I32, weights.shape, 0) + q_pos
                key = lax.broadcasted_iota(I32, weights.shape, 1) + (k_pos + tile * KEY_TILE)
                weights = jnp.where(keep(query, key), weights, 0.0)
            held = jnp.where(low, values, zero) if head == 0 else jnp.where(low, zero, values)
            term = jnp.dot(weights.astype(BF16), held, preferred_element_type=F32)
            total = term if total is None else total + term
        acc_ref[pl.ds(acc_at, rows), :] += total
        return carry

    lax.fori_loop(0, tiles, step, 0)


def from_before(query, key):
    return key >= query


def from_after(query, key):
    return key <= query


def read_lives(kv_ref, rows, group):
    code = kv_ref[pl.ds(rows, TAIL), :].astype(F32)
    return [
        (jnp.max(code[b : b + 1]) * TAIL + jnp.max(code[group + b : group + b + 1])).astype(I32)
        for b in range(group)
    ]


def spans(first, past, chunks):
    for index, (start, end) in enumerate(chunks):
        low, high = max(first, start), min(past, end)
        if low < high:
            yield index, low, high


def make_own(chunks, opening, block_rows, width):
    count = 1 if opening else len(chunks)
    group = chunks[-1][1]
    first_end = chunks[0][1]
    total = (first_end if opening else group) * block_rows

    def kernel(lives_ref, *refs):
        refs = list(refs)
        take = lambda number: [refs.pop(0) for _ in range(number)]
        queries = take(count)
        keys = take(count)
        if opening:
            (acc,) = take(1)
            acc[...] = jnp.zeros_like(acc)
        else:
            (old,) = take(1)
            acc, q_all = take(2)
            done = first_end * block_rows
            acc[pl.ds(0, done), :] = old[...]
            acc[pl.ds(done, total - done), :] = jnp.zeros((total - done, width), F32)
            for (low, high), ref in zip(chunks, queries):
                q_all[pl.ds(low * block_rows, (high - low) * block_rows), :] = ref[...]
        for k in range(first_end if opening else group):
            home = next(spans(k, k + 1, chunks))[0]
            start = 0 if opening or k >= first_end else first_end
            end = first_end if opening else group
            held = queries[0] if opening else q_all
            while start < end:
                past = min(start + 2, end)
                pair(
                    held,
                    start * block_rows,
                    start * block_rows,
                    keys[home],
                    (k - chunks[home][0]) * block_rows,
                    k * block_rows,
                    acc,
                    start * block_rows,
                    (past - start) * block_rows,
                    None,
                    lives_ref[k],
                    width,
                )
                start = past

    out = (jax.ShapeDtypeStruct((total, width), F32),)
    if not opening:
        out += (jax.ShapeDtypeStruct((total, 2 * width), BF16),)
    pairs = first_end**2 if opening else group**2 - first_end**2
    return pl.pallas_call(
        kernel,
        out_shape=out,
        in_specs=[SMEM_SPEC] + [VMEM_SPEC] * (2 * count + (0 if opening else 1)),
        out_specs=(VMEM_SPEC,) * len(out),
        compiler_params=limit(24),
        cost_estimate=cost(pairs * block_rows**2 * 2048, total * width * 8),
        name="own0" if opening else "own1",
    )


def make_turn(turn, chunks, block_rows, width):
    count = len(chunks)
    blocks = chunks[-1][1]
    head_rows = chunks[0][1] * block_rows

    def kernel(me_ref, *refs):
        before, after = refs[:count], refs[count : 2 * count]
        queries, old, out, acc = refs[2 * count :]
        q = lax.rem(me_ref[0] + 1 + turn, blocks)
        at = pl.multiple_of(q * block_rows, block_rows)
        lives_before = read_lives(before[0], head_rows, blocks)
        lives_after = read_lives(after[0], head_rows, blocks)
        acc[...] = old[pl.ds(at, block_rows), :]
        for k in range(blocks):
            home = next(spans(k, k + 1, chunks))[0]
            for held, keep, live in (
                (before, from_before, jnp.where(q <= k, lives_before[k], 0)),
                (after, from_after, jnp.where(q >= k, lives_after[k], 0)),
            ):
                pair(
                    queries,
                    at,
                    at,
                    held[home],
                    (k - chunks[home][0]) * block_rows,
                    k * block_rows,
                    acc,
                    0,
                    block_rows,
                    keep,
                    live,
                    width,
                )
        out[...] = acc[...].astype(BF16)

    return pl.pallas_call(
        kernel,
        out_shape=jax.ShapeDtypeStruct((block_rows, width), BF16),
        in_specs=[SMEM_SPEC] + [VMEM_SPEC] * (2 * count + 2),
        out_specs=VMEM_SPEC,
        scratch_shapes=[pltpu.VMEM((block_rows, width), F32)],
        compiler_params=limit(20),
        cost_estimate=cost(5 * block_rows**2 * 2048, block_rows * width * 8),
    )


def make_gate(group, chunks, rows, model_width, capacity):
    count = len(chunks)

    def kernel(me_ref, live_ref, *refs):
        candidates = refs[:count]
        gains, weights, domains, gating, emb_ref, slot_row, slot_col = refs[count:]
        me, live = me_ref[0], live_ref[0]
        for c in range(count):

            @pl.when((me >= chunks[c][0]) & (me < chunks[c][1]))
            def _():
                emb_ref[...] = candidates[c][...]

        position = lax.broadcasted_iota(I32, (rows, 1), 0)
        mask = (position < live).astype(F32)
        normed = (rms_norm(emb_ref[...].astype(F32), gains[0:1, :]) * mask).astype(BF16)
        gate = jnp.dot(normed, weights[...], preferred_element_type=F32)
        gating[...] = half_silu(gate * 0.5)
        turn = lax.rem(domains[...] - me + group, group)
        alive = lax.broadcasted_iota(I32, (1, rows), 1) < live
        expert = lax.broadcasted_iota(I32, (8, rows), 0)
        onehot = jnp.where((expert == turn) & alive, 1.0, 0.0)
        earlier = lax.broadcasted_iota(I32, (rows, rows), 0) < lax.broadcasted_iota(
            I32, (rows, rows), 1
        )
        rank = jnp.dot(
            onehot.astype(BF16),
            jnp.where(earlier, 1.0, 0.0).astype(BF16),
            preferred_element_type=F32,
        )
        slot = jnp.sum(onehot * (rank + (expert * capacity).astype(F32)), axis=0, keepdims=True)
        slot = jnp.where(alive, slot, -1.0)
        slot_row[...] = slot.astype(I32)
        slot_col[...] = jnp.transpose(jnp.broadcast_to(slot, (128, rows))).astype(I32)

    return pl.pallas_call(
        kernel,
        grid=(1,),
        out_shape=(
            jax.ShapeDtypeStruct((rows, model_width), F32),
            jax.ShapeDtypeStruct((rows, model_width), BF16),
            jax.ShapeDtypeStruct((1, rows), I32),
            jax.ShapeDtypeStruct((rows, 128), I32),
        ),
        in_specs=[SMEM_SPEC] * 2
        + [VMEM_SPEC] * (count + 1)
        + [pl.BlockSpec((model_width, model_width), lambda i: (0, 0)), VMEM_SPEC],
        out_specs=(VMEM_SPEC,) * 4,
        compiler_params=limit(12),
        cost_estimate=cost(2 * rows * model_width**2, 8 * rows * model_width),
        name="gate",
    )


def make_route(group, rows, width, model_width, capacity):
    def kernel(me_ref, *refs):
        pieces = refs[:group]
        gating, emb, gains, proj_out, slot = refs[group : group + 5]
        hidden_ref = refs[group + 5]
        sent = refs[group + 6 : group + 6 + group]
        att = refs[group + 6 + group]
        me = me_ref[0]
        for turn, piece in enumerate(pieces):
            column = lax.rem(me + group - 1 - turn, group)
            att[:, pl.ds(pl.multiple_of(column * width, width), width)] = piece[...].astype(F32)
        gated = (rms_norm(att[...], gains[1:2, :]) * gating[...]).astype(BF16)
        hidden = emb[...].astype(F32) + jnp.dot(
            gated, proj_out[...], preferred_element_type=F32
        )
        hidden_ref[...] = hidden
        routed = rms_norm(hidden, gains[2:3, :]).astype(BF16)
        for turn in range(group):
            place = lax.broadcasted_iota(I32, (capacity, rows), 0) + turn * capacity
            pick = jnp.where(place == slot[...], 1.0, 0.0).astype(BF16)
            sent[turn][...] = jnp.dot(pick, routed, preferred_element_type=F32).astype(BF16)

    return pl.pallas_call(
        kernel,
        out_shape=(jax.ShapeDtypeStruct((rows, model_width), F32),)
        + (jax.ShapeDtypeStruct((capacity, model_width), BF16),) * group,
        in_specs=[SMEM_SPEC] + [VMEM_SPEC] * (group + 5),
        out_specs=(VMEM_SPEC,) * (group + 1),
        scratch_shapes=[pltpu.VMEM((rows, model_width), F32)],
        compiler_params=limit(16),
        cost_estimate=cost(6 * rows * model_width**2, 8 * rows * model_width),
        name="route",
    )


def make_expert(rows, model_width, hidden):
    tile = hidden // 4

    def kernel(x, w_in, w_out, out):
        total = None
        for at in range(0, hidden, tile):
            gate = jnp.dot(x[...], w_in[0, :, at : at + tile], preferred_element_type=F32)
            up = jnp.dot(
                x[...], w_in[0, :, hidden + at : hidden + at + tile], preferred_element_type=F32
            )
            activated = (half_silu(gate * 0.5) * up).astype(BF16)
            term = jnp.dot(activated, w_out[0, at : at + tile, :], preferred_element_type=F32)
            total = term if total is None else total + term
        out[...] = total.astype(BF16)

    return pl.pallas_call(
        kernel,
        out_shape=jax.ShapeDtypeStruct((rows, model_width), BF16),
        in_specs=[VMEM_SPEC] * 3,
        out_specs=VMEM_SPEC,
        compiler_params=limit(16),
        cost_estimate=cost(6 * rows * model_width * hidden, 4 * rows * model_width),
        name="expert",
    )


def make_mix(group, rows, model_width, capacity):
    def kernel(live_ref, *refs):
        pieces = refs[:group]
        hidden, slot, out = refs[group:]
        total = hidden[...]
        where = slot[:, 0:1]
        for turn, piece in enumerate(pieces):
            place = lax.broadcasted_iota(I32, (rows, capacity), 1) + turn * capacity
            pick = jnp.where(place == where, 1.0, 0.0).astype(BF16)
            total = total + jnp.dot(pick, piece[...], preferred_element_type=F32)
        position = lax.broadcasted_iota(I32, (rows, 1), 0)
        mask = (position < live_ref[0]).astype(F32)
        out[...] = (mask * total).astype(BF16)

    return pl.pallas_call(
        kernel,
        out_shape=jax.ShapeDtypeStruct((rows, model_width), BF16),
        in_specs=[SMEM_SPEC] + [VMEM_SPEC] * (group + 2),
        out_specs=VMEM_SPEC,
        compiler_params=limit(12),
        cost_estimate=cost(2 * rows * rows * model_width * 2, 8 * rows * model_width),
        name="mix",
    )


def by_heads(
    item_ids, domains, live_counts, table, norm_gains, proj_in, proj_out, expert_in, expert_out
):
    group = lax.axis_size("emb")
    me = lax.axis_index("emb").astype(I32)[None]
    rows = domains.shape[0]
    model_width = proj_out.shape[0]
    hidden_units = expert_out.shape[1]
    width = model_width // group
    capacity = 2 * rows // group
    ends = [round(group * sum(CHUNKS[: c + 1])) for c in range(len(CHUNKS))]
    chunks = list(zip([0, *ends[:-1]], ends))

    high = lax.div(live_counts[0], TAIL)
    code = jnp.where(jnp.arange(TAIL, dtype=I32) < TAIL // 2, high, live_counts[0] - high * TAIL)
    code = jnp.broadcast_to(code.astype(BF16)[:, None], (TAIL, width))
    cut = chunks[0][1] * rows
    opening = jnp.concatenate((table[item_ids[:cut]], code))
    rest = table[item_ids[cut:]]
    mine = [opening] + [rest[a * rows - cut : b * rows - cut] for a, b in chunks[1:]]
    low, high, far = [], [], []
    for c, piece in enumerate(mine):
        low.append(rotated(piece, "emb", 1))
        high.append(rotated(piece, "emb", -1))
        far.append(rotated(low[c], "emb", 1))

    weights = make_weights(model_width, width)(me, proj_in, proj_in, proj_in)
    queries, own, before, after, candidates = [], [], [], [], []
    lives = acc = None
    for c, blocks in enumerate(chunks):
        project = make_project(group, blocks, rows, width, model_width)
        known = () if c == 0 else (lives,)
        pieces = (mine[c], low[c], high[c], far[c])
        if c == 1:
            pieces, acc = lax.optimization_barrier((pieces, acc))
        q, kv, emb, *more = project(me, *known, *pieces, norm_gains, weights)
        lives = more[0] if c == 0 else lives
        queries.append(q)
        own.append(kv)
        candidates.append(emb)
        before.append(shifted(kv, "seq", 1))
        after.append(shifted(kv, "seq", -1))
        if c == 0:
            (acc,) = make_own(chunks, True, rows, width)(lives, q, kv)
    acc, q_all = make_own(chunks, False, rows, width)(lives, *queries, *own, acc)

    gating, own_embedded, slot_row, slot_col = make_gate(
        group, chunks, rows, model_width, capacity
    )(me, live_counts, *candidates, norm_gains, proj_in, domains[None, :])

    pieces = []
    for t in range(group):
        turn = make_turn(t, chunks, rows, width)
        heads = turn(me, *before, *after, q_all, acc)
        if t < group - 1:
            heads = rotated(heads, "emb", t + 1)
        pieces.append(heads)
    route = make_route(group, rows, width, model_width, capacity)
    hidden, *sent = route(me, *pieces, gating, own_embedded, norm_gains, proj_out, slot_row)
    expert = make_expert(capacity, model_width, hidden_units)
    arrived = [sent[0]]
    for k in range(1, group):
        arrived.append(rotated(sent[k], "emb", k))
    returned = []
    for k in range(group):
        made = expert(arrived[k], expert_in, expert_out)
        if k > 0:
            made = rotated(made, "emb", -k)
        returned.append(made)
    mix = make_mix(group, rows, model_width, capacity)
    return mix(live_counts, *returned, hidden, slot_col)


def by_rows(
    item_ids, domains, live_counts, table, norm_gains, proj_in, proj_out, expert_in, expert_out
):
    rows_dev = domains.shape[0]
    model_width = proj_out.shape[0]
    hidden_units = expert_out.shape[1]
    group_size = lax.axis_size("emb")
    capacity = 2 * rows_dev // group_size
    columns = table[item_ids]
    embedded = lax.all_to_all(columns, "emb", split_axis=0, concat_axis=1, tiled=True).astype(
        jnp.float32
    )
    positions = jnp.arange(rows_dev, dtype=jnp.int32)
    live_mask = (positions < live_counts[0]).astype(jnp.float32)
    normed = (rms_norm(embedded, norm_gains[0]) * live_mask[:, None]).astype(jnp.bfloat16)
    projected = jnp.dot(normed, proj_in, preferred_element_type=jnp.float32)
    gating = jax.nn.silu(projected[:, :model_width])
    queries = (
        projected[:, model_width : 2 * model_width]
        .astype(jnp.bfloat16)
        .reshape(rows_dev, HEADS, HEAD_DIM)
    )
    own_pair = jnp.stack(
        (
            projected[:, 2 * model_width : 3 * model_width].astype(jnp.bfloat16),
            projected[:, 3 * model_width :].astype(jnp.bfloat16),
        )
    )
    key_weights = proj_in[:, 2 * model_width :]
    upper_band = positions[None, :] >= positions[:, None]
    lower_band = positions[None, :] <= positions[:, None]
    score_scale = 1.0 / math.sqrt(HEAD_DIM)

    def unpack(piece):
        rebuilt = jnp.dot(piece[0], key_weights, preferred_element_type=jnp.float32)
        return jnp.stack(
            (
                rebuilt[:, :model_width].astype(jnp.bfloat16),
                rebuilt[:, model_width:].astype(jnp.bfloat16),
            )
        )

    def attend(both, band_mask):
        key_heads = both[0].reshape(rows_dev, HEADS, HEAD_DIM)
        value_heads = both[1].reshape(rows_dev, HEADS, HEAD_DIM)
        scores = (
            jnp.einsum("qhd,khd->hqk", queries, key_heads, preferred_element_type=jnp.float32)
            * score_scale
        )
        weights = jax.nn.silu(scores)
        if band_mask is not None:
            weights = jnp.where(band_mask[None], weights, 0.0)
        weights = weights.astype(jnp.bfloat16)
        return jnp.einsum(
            "hqk,khd->qhd", weights, value_heads, preferred_element_type=jnp.float32
        ).reshape(rows_dev, model_width)

    outgoing = normed[None]
    attended = attend(own_pair, None)
    for distance in range(1, SPAN + 1):
        band_before = upper_band if distance == SPAN else None
        band_after = lower_band if distance == SPAN else None
        earlier = shifted(outgoing, ("seq", "emb"), distance)
        following = shifted(outgoing, ("seq", "emb"), -distance)
        attended = (
            attended + attend(unpack(earlier), band_before) + attend(unpack(following), band_after)
        )
    gated = (rms_norm(attended, norm_gains[1]) * gating).astype(jnp.bfloat16)
    hidden = embedded + jnp.dot(gated, proj_out, preferred_element_type=jnp.float32)
    routed = rms_norm(hidden, norm_gains[2]).astype(jnp.bfloat16)
    onehot_domain = (domains[:, None] == jnp.arange(group_size, dtype=jnp.int32)[None, :]).astype(
        jnp.int32
    )
    slot_rank = jnp.sum((jnp.cumsum(onehot_domain, axis=0) - onehot_domain) * onehot_domain, axis=1)
    slot_index = domains * capacity + slot_rank
    outgoing_rows = (
        jnp.zeros((group_size * capacity, model_width), jnp.bfloat16).at[slot_index].set(routed)
    )
    outgoing_rows = outgoing_rows.reshape(group_size, capacity, model_width)
    inbox = lax.all_to_all(outgoing_rows, "emb", split_axis=0, concat_axis=0, tiled=True)
    sources, slot_count, _ = inbox.shape
    flattened = inbox.reshape(sources * slot_count, model_width)
    gate_up = jnp.dot(flattened, expert_in[0], preferred_element_type=jnp.float32)
    activated = (jax.nn.silu(gate_up[:, :hidden_units]) * gate_up[:, hidden_units:]).astype(
        jnp.bfloat16
    )
    produced = jnp.dot(activated, expert_out[0], preferred_element_type=jnp.float32).astype(
        jnp.bfloat16
    )
    finished = produced.reshape(sources, slot_count, model_width)
    returned = lax.all_to_all(finished, "emb", split_axis=0, concat_axis=0, tiled=True).reshape(
        group_size * capacity, model_width
    )
    expert_rows = returned[slot_index].astype(jnp.float32)
    return (live_mask[:, None] * (hidden + expert_rows)).astype(jnp.bfloat16)


def solution(mesh):
    group = mesh.shape["emb"]
    split_heads = group == SPAN and HEADS == 2 * group

    def body(*arrays):
        return (by_heads if split_heads else by_rows)(*arrays)

    in_specs = (
        P("seq"),
        P(("seq", "emb")),
        P(("seq", "emb")),
        P(None, "emb"),
        P(),
        P(),
        P(),
        P("emb", None, None),
        P("emb", None, None),
    )
    out_specs = P(("seq", "emb"), None)
    return jax.shard_map(body, mesh=mesh, in_specs=in_specs, out_specs=out_specs, check_vma=False)
```

```python
import functools
import math

import jax
import jax.numpy as jnp
from jax import lax
from jax.experimental import pallas as pl
from jax.experimental.pallas import tpu as pltpu
from jax.sharding import PartitionSpec as P


HEADS = 8
HEAD_DIM = 64
SPAN = 4
NORM_EPS = 1e-06
CHUNKS = (0.25, 0.25, 0.5)
KEY_TILE = 256
TAIL = 16
MIB = 1 << 20

F32 = jnp.float32
BF16 = jnp.bfloat16
I32 = jnp.int32


def shifted(value, axis, steps):
    count = lax.axis_size(axis)
    first, last = (max(0, -steps), min(count, count - steps))
    return lax.ppermute(value, axis, [(source, source + steps) for source in range(first, last)])


def rotated(value, axis, steps):
    count = lax.axis_size(axis)
    return lax.ppermute(value, axis, [(source, (source + steps) % count) for source in range(count)])


def rms_norm(values, gain):
    return values * lax.rsqrt(jnp.mean(values * values, axis=-1, keepdims=True) + NORM_EPS) * gain


def half_silu(half):
    return half + half * jnp.tanh(half)


VMEM_SPEC = pl.BlockSpec(memory_space=pltpu.VMEM)
SMEM_SPEC = pl.BlockSpec(memory_space=pltpu.SMEM)


def cost(flops, nbytes):
    return pl.CostEstimate(flops=int(flops), bytes_accessed=int(nbytes), transcendentals=0)


def limit(mib):
    return pltpu.CompilerParams(vmem_limit_bytes=mib * MIB)


def make_weights(model_width, width):
    def kernel(me, w_q, w_k, w_v, out):
        queries = w_q[...]
        low = lax.broadcasted_iota(I32, queries.shape, 1) < HEAD_DIM
        zero = jnp.zeros_like(queries)
        out[:, :width] = jnp.where(low, queries, zero)
        out[:, width : 2 * width] = jnp.where(low, zero, queries)
        out[:, 2 * width : 3 * width] = w_k[...]
        out[:, 3 * width :] = w_v[...]

    per = model_width // width
    block = lambda index: pl.BlockSpec(
        (model_width, width), lambda i, me: (0, index * per + me[0])
    )
    return pl.pallas_call(
        kernel,
        grid_spec=pltpu.PrefetchScalarGridSpec(
            num_scalar_prefetch=1,
            grid=(1,),
            in_specs=[block(1), block(2), block(3)],
            out_specs=pl.BlockSpec((model_width, 4 * width), lambda i, me: (0, 0)),
        ),
        out_shape=jax.ShapeDtypeStruct((model_width, 4 * width), BF16),
        compiler_params=limit(4),
        cost_estimate=cost(0, 16 * model_width * width),
        name="weights",
    )


def make_project(group, blocks, block_rows, width, model_width):
    lane = model_width // group
    first, past = blocks
    per = past - first
    rows = per * block_rows
    opening = first == 0

    def kernel(me_ref, *refs):
        refs = list(refs)
        take = lambda number: [refs.pop(0) for _ in range(number)]
        known = None if opening else take(1)[0]
        pieces = take(group)
        gains, weights = take(2)
        q_ref, kv_ref, emb_ref = take(3)
        lives_ref = take(1)[0] if opening else None
        me = me_ref[0]
        offsets = (0, group - 1, 1, 2)
        for piece, offset in zip(pieces, offsets):
            column = lax.rem(me + offset, group)
            emb_ref[:, pl.ds(pl.multiple_of(column * lane, lane), lane)] = piece[pl.ds(0, rows), :]
            if opening:
                code = piece[rows : rows + TAIL, :].astype(F32)
                high, low = (jnp.max(code[at : at + 1]) for at in (TAIL - 2, TAIL - 1))
                lives_ref[column] = (high * TAIL + low).astype(I32)
        lives = [(lives_ref if opening else known)[b] for b in range(group)]
        for part in range(per):
            here = pl.ds(part * block_rows, block_rows)
            position = lax.broadcasted_iota(I32, (block_rows, 1), 0)
            mask = (position < lives[first + part]).astype(F32)
            embedded = emb_ref[here, :].astype(F32)
            normed = (rms_norm(embedded, gains[0:1, :]) * mask).astype(BF16)
            projected = jnp.dot(normed, weights[...], preferred_element_type=F32)
            scale = 0.5 / math.sqrt(HEAD_DIM)
            q_ref[here, :] = projected[:, : 2 * width].astype(BF16) * jnp.asarray(scale, BF16)
            kv_ref[here, :] = projected[:, 2 * width :].astype(BF16)
        if opening:
            row = lax.broadcasted_iota(I32, (TAIL, 2 * width), 0)
            code = jnp.zeros((TAIL, 2 * width), F32)
            for b in range(group):
                high = lax.div(lives[b], TAIL)
                code = jnp.where(row == b, high.astype(F32), code)
                code = jnp.where(row == group + b, (lives[b] - high * TAIL).astype(F32), code)
            kv_ref[pl.ds(rows, TAIL), :] = code.astype(BF16)

    more = TAIL if opening else 0
    out_shape = (
        jax.ShapeDtypeStruct((rows, 2 * width), BF16),
        jax.ShapeDtypeStruct((rows + more, 2 * width), BF16),
        jax.ShapeDtypeStruct((rows, model_width), BF16),
    )
    out_specs = (VMEM_SPEC,) * 3
    if opening:
        out_shape += (jax.ShapeDtypeStruct((group,), I32),)
        out_specs += (SMEM_SPEC,)
    return pl.pallas_call(
        kernel,
        out_shape=out_shape,
        in_specs=[SMEM_SPEC] * (1 if opening else 2) + [VMEM_SPEC] * (group + 2),
        out_specs=out_specs,
        compiler_params=limit(16),
        cost_estimate=cost(2 * rows * model_width * 4 * width, 4 * rows * model_width),
    )


def pair(queries, q_at, q_pos, kv_ref, k_at, k_pos, acc_ref, acc_at, rows, keep, live, width):
    tiles = lax.div(live + (KEY_TILE - 1), KEY_TILE)

    def step(tile, carry):
        at = pl.ds(pl.multiple_of(k_at + tile * KEY_TILE, KEY_TILE), KEY_TILE)
        keys = kv_ref[at, :width]
        values = kv_ref[at, width:]
        low = lax.broadcasted_iota(I32, values.shape, 1) < HEAD_DIM
        zero = jnp.zeros_like(values)
        total = None
        for head in range(2):
            half = lax.dot_general(
                queries[pl.ds(q_at, rows), head * width : (head + 1) * width],
                keys,
                (((1,), (1,)), ((), ())),
                preferred_element_type=F32,
            )
            weights = half_silu(half)
            if keep is not None:
                query = lax.broadcasted_iota(I32, weights.shape, 0) + q_pos
                key = lax.broadcasted_iota(I32, weights.shape, 1) + (k_pos + tile * KEY_TILE)
                weights = jnp.where(keep(query, key), weights, 0.0)
            held = jnp.where(low, values, zero) if head == 0 else jnp.where(low, zero, values)
            term = jnp.dot(weights.astype(BF16), held, preferred_element_type=F32)
            total = term if total is None else total + term
        acc_ref[pl.ds(acc_at, rows), :] += total
        return carry

    lax.fori_loop(0, tiles, step, 0)


def from_before(query, key):
    return key >= query


def from_after(query, key):
    return key <= query


def read_lives(kv_ref, rows, group):
    code = kv_ref[pl.ds(rows, TAIL), :].astype(F32)
    return [
        (jnp.max(code[b : b + 1]) * TAIL + jnp.max(code[group + b : group + b + 1])).astype(I32)
        for b in range(group)
    ]


def spans(first, past, chunks):
    for index, (start, end) in enumerate(chunks):
        low, high = max(first, start), min(past, end)
        if low < high:
            yield index, low, high


def make_own(chunks, opening, block_rows, width):
    group = chunks[-1][1]
    first_end = chunks[-1][0]
    parts = chunks[:-1] if opening else [(0, first_end), chunks[-1]]
    blocks = first_end if opening else group
    done = 0 if opening else first_end * block_rows
    total = blocks * block_rows

    def kernel(lives_ref, *refs):
        refs = list(refs)
        take = lambda number: [refs.pop(0) for _ in range(number)]
        queries = take(len(parts))
        keys = take(len(chunks) - 1 if opening else len(chunks))
        old = None if opening else take(1)[0]
        acc, q_all = take(2)
        if not opening:
            acc[pl.ds(0, done), :] = old[...]
        acc[pl.ds(done, total - done), :] = jnp.zeros((total - done, width), F32)
        for (low, high), ref in zip(parts, queries):
            q_all[pl.ds(low * block_rows, (high - low) * block_rows), :] = ref[...]
        for k in range(blocks):
            home = next(spans(k, k + 1, chunks))[0]
            start = 0 if opening or k >= first_end else first_end
            while start < blocks:
                past = min(start + 2, blocks)
                pair(
                    q_all,
                    start * block_rows,
                    start * block_rows,
                    keys[home],
                    (k - chunks[home][0]) * block_rows,
                    k * block_rows,
                    acc,
                    start * block_rows,
                    (past - start) * block_rows,
                    None,
                    lives_ref[k],
                    width,
                )
                start = past

    inputs = len(parts) + (len(chunks) - 1 if opening else len(chunks) + 1)
    pairs = first_end**2 if opening else group**2 - first_end**2
    return pl.pallas_call(
        kernel,
        out_shape=(
            jax.ShapeDtypeStruct((total, width), F32),
            jax.ShapeDtypeStruct((total, 2 * width), BF16),
        ),
        in_specs=[SMEM_SPEC] + [VMEM_SPEC] * inputs,
        out_specs=(VMEM_SPEC,) * 2,
        compiler_params=limit(24),
        cost_estimate=cost(pairs * block_rows**2 * 2048, total * width * 8),
        name="own0" if opening else "own1",
    )


def make_near(c, chunks, block_rows, width):
    first, past = chunks[c]
    known = chunks[-1][0]
    head_rows = chunks[0][1] * block_rows

    def kernel(*refs):
        before, after = refs[:2]
        heads = refs[2:-3] or (before, after)
        queries, old, acc = refs[-3:]
        acc[...] = old[...]
        lives_before = read_lives(heads[0], head_rows, chunks[-1][1])
        lives_after = read_lives(heads[1], head_rows, chunks[-1][1])
        for k in range(first, past):
            jobs = [(before, 0, k, None), (before, k, k + 1, from_before)]
            jobs += [(after, k, k + 1, from_after), (after, k + 1, known, None)]
            for held, low, high, keep in jobs:
                if low == high:
                    continue
                pair(
                    queries,
                    low * block_rows,
                    low * block_rows,
                    held,
                    (k - first) * block_rows,
                    k * block_rows,
                    acc,
                    low * block_rows,
                    (high - low) * block_rows,
                    keep,
                    (lives_before if held is before else lives_after)[k],
                    width,
                )

    operands = 4 if c == 0 else 6
    return pl.pallas_call(
        kernel,
        out_shape=jax.ShapeDtypeStruct((known * block_rows, width), F32),
        in_specs=[VMEM_SPEC] * operands,
        out_specs=VMEM_SPEC,
        input_output_aliases={operands - 1: 0},
        compiler_params=limit(20),
        cost_estimate=cost(3 * block_rows**2 * 2048, known * block_rows * width * 8),
    )


def make_last(batch, chunks, block_rows, width, capacity):
    count = len(chunks)
    first, blocks = chunks[-1]
    head_rows = chunks[0][1] * block_rows
    size = len(batch) * capacity

    def kernel(*refs):
        after = refs[:count]
        before, first_before = refs[count : count + 2]
        queries, old, slots = refs[count + 2 : count + 5]
        out = refs[count + 5 : -1]
        acc = refs[-1]
        lives_before = read_lives(first_before, head_rows, blocks)
        lives_after = read_lives(after[0], head_rows, blocks)
        for order, q in enumerate(batch):
            at = q * block_rows
            acc[...] = old[pl.ds(at, block_rows), :]

            def run(held, k, keep, live):
                start = chunks[next(spans(k, k + 1, chunks))[0]][0]
                pair(
                    queries,
                    at,
                    at,
                    held,
                    (k - start) * block_rows,
                    k * block_rows,
                    acc,
                    0,
                    block_rows,
                    keep,
                    live,
                    width,
                )

            for k in range(blocks):
                home = next(spans(k, k + 1, chunks))[0]
                if k >= first and q <= k:
                    run(before, k, from_before if q == k else None, lives_before[k])
                if q >= first and q >= k:
                    run(after[home], k, from_after if q == k else None, lives_after[k])
            attended = acc[...].astype(BF16)
            for turn in range(blocks):
                place = lax.broadcasted_iota(I32, (capacity, block_rows), 0) + turn * capacity
                pick = jnp.where(place == slots[q : q + 1, :], 1.0, 0.0).astype(BF16)
                out[turn][pl.ds(order * capacity, capacity), :] = jnp.dot(
                    pick, attended, preferred_element_type=F32
                ).astype(BF16)

    return pl.pallas_call(
        kernel,
        out_shape=(jax.ShapeDtypeStruct((size, width), BF16),) * blocks,
        in_specs=[VMEM_SPEC] * (count + 5),
        out_specs=(VMEM_SPEC,) * blocks,
        scratch_shapes=[pltpu.VMEM((block_rows, width), F32)],
        compiler_params=limit(20),
        cost_estimate=cost(7 * block_rows**2 * 2048, block_rows * width * 16),
    )


def make_slots(group, block_rows, capacity):
    lanes = 128
    strips = block_rows // lanes

    def kernel(me_ref, lives_ref, *refs):
        pieces = refs[:group]
        slots, slot_col = refs[group:]
        me = me_ref[0]
        earlier = lax.broadcasted_iota(I32, (block_rows, block_rows), 0) < lax.broadcasted_iota(
            I32, (block_rows, block_rows), 1
        )
        earlier = jnp.where(earlier, 1.0, 0.0).astype(BF16)
        position = lax.broadcasted_iota(I32, (1, block_rows), 1)
        expert = lax.broadcasted_iota(I32, (8, block_rows), 0)
        for piece, offset in zip(pieces, (0, group - 1, 1, 2)):
            block = lax.rem(me + offset, group)
            code = piece[pl.ds(block_rows, TAIL), :].astype(F32)
            domain = jnp.concatenate([code[r : r + 1, :] for r in range(strips)], axis=1)
            turn = domain.astype(I32) - me
            turn = jnp.where(turn < 0, turn + group, turn)
            alive = position < lives_ref[block]
            onehot = jnp.where((expert == turn) & alive, 1.0, 0.0)
            rank = jnp.dot(onehot.astype(BF16), earlier, preferred_element_type=F32)
            slot = jnp.sum(
                onehot * (rank + (expert * capacity).astype(F32)), axis=0, keepdims=True
            )
            slot = jnp.where(alive, slot, -1.0)
            slots[pl.ds(block, 1), :] = slot.astype(I32)
            if offset == 0:
                slot_col[...] = jnp.transpose(jnp.broadcast_to(slot, (lanes, block_rows))).astype(
                    I32
                )

    return pl.pallas_call(
        kernel,
        out_shape=(
            jax.ShapeDtypeStruct((8, block_rows), I32),
            jax.ShapeDtypeStruct((block_rows, lanes), I32),
        ),
        in_specs=[SMEM_SPEC] * 2 + [VMEM_SPEC] * group,
        out_specs=(VMEM_SPEC,) * 2,
        compiler_params=limit(12),
        cost_estimate=cost(2 * 32 * block_rows**2, 8 * block_rows * lanes),
        name="slots",
    )


def make_select(batch, chunks, block_rows, model_width, capacity):
    homes = [next(spans(b, b + 1, chunks))[0] for b in batch]
    size = len(batch) * capacity

    def kernel(*refs):
        sources = refs[: len(batch)]
        slots, gains, weights, emb, gating = refs[len(batch) :]
        for order, (b, home, source) in enumerate(zip(batch, homes, sources)):
            place = lax.broadcasted_iota(I32, (capacity, block_rows), 0)
            pick = jnp.where(place == slots[b : b + 1, :], 1.0, 0.0).astype(BF16)
            rows = source[pl.ds((b - chunks[home][0]) * block_rows, block_rows), :]
            emb[pl.ds(order * capacity, capacity), :] = jnp.dot(
                pick, rows, preferred_element_type=F32
            ).astype(BF16)
        normed = rms_norm(emb[...].astype(F32), gains[0:1, :]).astype(BF16)
        gate = jnp.dot(normed, weights[...], preferred_element_type=F32)
        gating[...] = half_silu(gate * 0.5)

    return homes, pl.pallas_call(
        kernel,
        grid=(1,),
        out_shape=(
            jax.ShapeDtypeStruct((size, model_width), BF16),
            jax.ShapeDtypeStruct((size, model_width), F32),
        ),
        in_specs=[VMEM_SPEC] * (len(batch) + 2)
        + [pl.BlockSpec((model_width, model_width), lambda i: (0, 0))],
        out_specs=(VMEM_SPEC,) * 2,
        compiler_params=limit(12),
        cost_estimate=cost(4 * size * model_width**2, 8 * size * model_width),
    )


def make_serve(batch, senders, group, width, model_width, hidden_units, capacity):
    size = len(batch) * capacity
    tile = hidden_units // 4

    def kernel(me_ref, *refs):
        pieces = refs[:group]
        emb, gating, gains, proj_out, w_in, w_out = refs[group : group + 6]
        out = refs[group + 6 : -2]
        att, done = refs[-2:]
        me = me_ref[0]
        for k, piece in enumerate(pieces):
            column = lax.rem(me + group - k, group)
            att[:, pl.ds(pl.multiple_of(column * width, width), width)] = piece[...].astype(F32)
        gated = (rms_norm(att[...], gains[1:2, :]) * gating[...]).astype(BF16)
        hidden = emb[...].astype(F32) + jnp.dot(
            gated, proj_out[...], preferred_element_type=F32
        )
        routed = rms_norm(hidden, gains[2:3, :]).astype(BF16)
        total = None
        for at in range(0, hidden_units, tile):
            gate = jnp.dot(routed, w_in[0, :, at : at + tile], preferred_element_type=F32)
            up = jnp.dot(
                routed,
                w_in[0, :, hidden_units + at : hidden_units + at + tile],
                preferred_element_type=F32,
            )
            activated = (half_silu(gate * 0.5) * up).astype(BF16)
            term = jnp.dot(activated, w_out[0, at : at + tile, :], preferred_element_type=F32)
            total = term if total is None else total + term
        done[...] = (hidden + total.astype(BF16).astype(F32)).astype(BF16)
        for ref, sender in zip(out, (*senders, batch[0])):
            at = jnp.where(me == sender, 0, capacity)
            ref[...] = done[pl.ds(pl.multiple_of(at, capacity), capacity), :]

    return pl.pallas_call(
        kernel,
        out_shape=(jax.ShapeDtypeStruct((capacity, model_width), BF16),) * (len(senders) + 1),
        in_specs=[SMEM_SPEC] + [VMEM_SPEC] * (group + 6),
        out_specs=(VMEM_SPEC,) * (len(senders) + 1),
        scratch_shapes=[
            pltpu.VMEM((size, model_width), F32),
            pltpu.VMEM((size, model_width), BF16),
        ],
        compiler_params=limit(20),
        cost_estimate=cost(6 * size * model_width * hidden_units, 8 * size * model_width),
    )


def make_mix(group, exchanges, rows, model_width, capacity):
    def kernel(me_ref, *refs):
        pieces, (slot, out) = refs[:-2], refs[-2:]
        me = me_ref[0]
        where = slot[:, 0:1]
        per = len(pieces) // 2
        first = functools.reduce(
            jnp.logical_or, [me == target for _, target in exchanges[0][0]]
        )
        total = None
        for j in range(per):
            piece = jnp.where(
                lax.broadcasted_iota(I32, (capacity, model_width), 0) * 0 + first.astype(I32) > 0,
                pieces[j][...].astype(F32),
                pieces[per + j][...].astype(F32),
            ).astype(BF16)
            turn = jnp.zeros_like(me)
            if j < per - 1:
                for exchange in exchanges:
                    for source, target in exchange[j]:
                        turn = jnp.where(me == target, (source - target) % group, turn)
            place = lax.broadcasted_iota(I32, (rows, capacity), 1) + turn * capacity
            pick = jnp.where(place == where, 1.0, 0.0).astype(BF16)
            term = jnp.dot(pick, piece, preferred_element_type=F32)
            total = term if total is None else total + term
        out[...] = total.astype(BF16)

    return pl.pallas_call(
        kernel,
        out_shape=jax.ShapeDtypeStruct((rows, model_width), BF16),
        in_specs=[SMEM_SPEC] + [VMEM_SPEC] * (2 * (len(exchanges[0]) + 1) + 1),
        out_specs=VMEM_SPEC,
        compiler_params=limit(16),
        cost_estimate=cost(4 * rows * rows * model_width, 8 * rows * model_width),
        name="mix",
    )


BATCHES = ((0, 3), (1, 2))
HOMEWARD = (
    (((1, 0), (2, 3)), ((2, 0), (1, 3)), ((3, 0), (0, 3))),
    (((0, 1), (3, 2)), ((2, 1), (1, 2)), ((3, 1), (0, 2))),
)


def by_heads(
    item_ids, domains, live_counts, table, norm_gains, proj_in, proj_out, expert_in, expert_out
):
    group = lax.axis_size("emb")
    me = lax.axis_index("emb").astype(I32)[None]
    rows = domains.shape[0]
    model_width = proj_out.shape[0]
    hidden_units = expert_out.shape[1]
    width = model_width // group
    capacity = 2 * rows // group
    ends = [round(group * sum(CHUNKS[: c + 1])) for c in range(len(CHUNKS))]
    chunks = list(zip([0, *ends[:-1]], ends))

    high = lax.div(live_counts[0], TAIL)
    count_code = jnp.stack((high, live_counts[0] - high * TAIL))
    code = jnp.concatenate(
        (
            domains.reshape(rows // width, width),
            jnp.zeros((TAIL - 2 - rows // width, width), I32),
            jnp.broadcast_to(count_code[:, None], (2, width)),
        )
    ).astype(BF16)
    cut = chunks[0][1] * rows
    opening = jnp.concatenate((table[item_ids[:cut]], code))
    rest = table[item_ids[cut:]]
    mine = [opening] + [rest[a * rows - cut : b * rows - cut] for a, b in chunks[1:]]
    low, high, far = [], [], []
    for c, piece in enumerate(mine):
        low.append(rotated(piece, "emb", 1))
        high.append(rotated(piece, "emb", -1))
        far.append(rotated(low[c], "emb", 1))

    weights = make_weights(model_width, width)(me, proj_in, proj_in, proj_in)
    queries, own, before, after, embedded = [], [], [], [], []
    lives = acc = None
    for c, blocks in enumerate(chunks):
        project = make_project(group, blocks, rows, width, model_width)
        known = () if c == 0 else (lives,)
        pieces = (mine[c], low[c], high[c], far[c])
        q, kv, emb, *more = project(me, *known, *pieces, norm_gains, weights)
        if c == 0:
            lives = more[0]
            slots, slot_col = make_slots(group, rows, capacity)(me, lives, *pieces)
        queries.append(q)
        own.append(kv)
        embedded.append(emb)
        before.append(shifted(kv, "seq", 1))
        after.append(shifted(kv, "seq", -1))
        if c == len(chunks) - 2:
            acc, q_all = make_own(chunks, True, rows, width)(lives, *queries, *own)
    for c in range(len(chunks) - 1):
        heads = () if c == 0 else (before[0], after[0])
        acc = make_near(c, chunks, rows, width)(before[c], after[c], *heads, q_all, acc)
    acc, q_all = make_own(chunks, False, rows, width)(lives, q_all, queries[-1], *own, acc)

    sent = []
    for batch in BATCHES:
        last = make_last(batch, chunks, rows, width, capacity)
        shares = last(*after, before[-1], before[0], q_all, acc, slots)
        arrived = [shares[0]]
        for k in range(1, group):
            arrived.append(rotated(shares[k], "emb", k))
        sent.append(arrived)
    finished = []
    for n, batch in enumerate(BATCHES):
        homes, select = make_select(batch, chunks, rows, model_width, capacity)
        emb, gating = select(*(embedded[h] for h in homes), slots, norm_gains, proj_in)
        senders = [source for pairs in HOMEWARD[n] for source, target in pairs[:1]]
        serve = make_serve(batch, senders, group, width, model_width, hidden_units, capacity)
        made = serve(
            me, *sent[n], emb, gating, norm_gains, proj_out, expert_in, expert_out
        )
        for j, pairs in enumerate(HOMEWARD[n]):
            finished.append(lax.ppermute(made[j], "emb", pairs))
        finished.append(made[-1])
    mix = make_mix(group, HOMEWARD, rows, model_width, capacity)
    return mix(me, *finished, slot_col)


def by_rows(
    item_ids, domains, live_counts, table, norm_gains, proj_in, proj_out, expert_in, expert_out
):
    rows_dev = domains.shape[0]
    model_width = proj_out.shape[0]
    hidden_units = expert_out.shape[1]
    group_size = lax.axis_size("emb")
    capacity = 2 * rows_dev // group_size
    columns = table[item_ids]
    embedded = lax.all_to_all(columns, "emb", split_axis=0, concat_axis=1, tiled=True).astype(
        jnp.float32
    )
    positions = jnp.arange(rows_dev, dtype=jnp.int32)
    live_mask = (positions < live_counts[0]).astype(jnp.float32)
    normed = (rms_norm(embedded, norm_gains[0]) * live_mask[:, None]).astype(jnp.bfloat16)
    projected = jnp.dot(normed, proj_in, preferred_element_type=jnp.float32)
    gating = jax.nn.silu(projected[:, :model_width])
    queries = (
        projected[:, model_width : 2 * model_width]
        .astype(jnp.bfloat16)
        .reshape(rows_dev, HEADS, HEAD_DIM)
    )
    own_pair = jnp.stack(
        (
            projected[:, 2 * model_width : 3 * model_width].astype(jnp.bfloat16),
            projected[:, 3 * model_width :].astype(jnp.bfloat16),
        )
    )
    key_weights = proj_in[:, 2 * model_width :]
    upper_band = positions[None, :] >= positions[:, None]
    lower_band = positions[None, :] <= positions[:, None]
    score_scale = 1.0 / math.sqrt(HEAD_DIM)

    def unpack(piece):
        rebuilt = jnp.dot(piece[0], key_weights, preferred_element_type=jnp.float32)
        return jnp.stack(
            (
                rebuilt[:, :model_width].astype(jnp.bfloat16),
                rebuilt[:, model_width:].astype(jnp.bfloat16),
            )
        )

    def attend(both, band_mask):
        key_heads = both[0].reshape(rows_dev, HEADS, HEAD_DIM)
        value_heads = both[1].reshape(rows_dev, HEADS, HEAD_DIM)
        scores = (
            jnp.einsum("qhd,khd->hqk", queries, key_heads, preferred_element_type=jnp.float32)
            * score_scale
        )
        weights = jax.nn.silu(scores)
        if band_mask is not None:
            weights = jnp.where(band_mask[None], weights, 0.0)
        weights = weights.astype(jnp.bfloat16)
        return jnp.einsum(
            "hqk,khd->qhd", weights, value_heads, preferred_element_type=jnp.float32
        ).reshape(rows_dev, model_width)

    outgoing = normed[None]
    attended = attend(own_pair, None)
    for distance in range(1, SPAN + 1):
        band_before = upper_band if distance == SPAN else None
        band_after = lower_band if distance == SPAN else None
        earlier = shifted(outgoing, ("seq", "emb"), distance)
        following = shifted(outgoing, ("seq", "emb"), -distance)
        attended = (
            attended + attend(unpack(earlier), band_before) + attend(unpack(following), band_after)
        )
    gated = (rms_norm(attended, norm_gains[1]) * gating).astype(jnp.bfloat16)
    hidden = embedded + jnp.dot(gated, proj_out, preferred_element_type=jnp.float32)
    routed = rms_norm(hidden, norm_gains[2]).astype(jnp.bfloat16)
    onehot_domain = (domains[:, None] == jnp.arange(group_size, dtype=jnp.int32)[None, :]).astype(
        jnp.int32
    )
    slot_rank = jnp.sum((jnp.cumsum(onehot_domain, axis=0) - onehot_domain) * onehot_domain, axis=1)
    slot_index = domains * capacity + slot_rank
    outgoing_rows = (
        jnp.zeros((group_size * capacity, model_width), jnp.bfloat16).at[slot_index].set(routed)
    )
    outgoing_rows = outgoing_rows.reshape(group_size, capacity, model_width)
    inbox = lax.all_to_all(outgoing_rows, "emb", split_axis=0, concat_axis=0, tiled=True)
    sources, slot_count, _ = inbox.shape
    flattened = inbox.reshape(sources * slot_count, model_width)
    gate_up = jnp.dot(flattened, expert_in[0], preferred_element_type=jnp.float32)
    activated = (jax.nn.silu(gate_up[:, :hidden_units]) * gate_up[:, hidden_units:]).astype(
        jnp.bfloat16
    )
    produced = jnp.dot(activated, expert_out[0], preferred_element_type=jnp.float32).astype(
        jnp.bfloat16
    )
    finished = produced.reshape(sources, slot_count, model_width)
    returned = lax.all_to_all(finished, "emb", split_axis=0, concat_axis=0, tiled=True).reshape(
        group_size * capacity, model_width
    )
    expert_rows = returned[slot_index].astype(jnp.float32)
    return (live_mask[:, None] * (hidden + expert_rows)).astype(jnp.bfloat16)


def solution(mesh):
    group = mesh.shape["emb"]
    split_heads = group == SPAN and HEADS == 2 * group

    def body(*arrays):
        return (by_heads if split_heads else by_rows)(*arrays)

    in_specs = (
        P("seq"),
        P(("seq", "emb")),
        P(("seq", "emb")),
        P(None, "emb"),
        P(),
        P(),
        P(),
        P("emb", None, None),
        P("emb", None, None),
    )
    out_specs = P(("seq", "emb"), None)
    return jax.shard_map(body, mesh=mesh, in_specs=in_specs, out_specs=out_specs, check_vma=False)
```

```python
import functools
import math

import jax
import jax.numpy as jnp
from jax import lax
from jax.experimental import pallas as pl
from jax.experimental.pallas import tpu as pltpu
from jax.sharding import PartitionSpec as P


HEADS = 8
HEAD_DIM = 64
SPAN = 4
NORM_EPS = 1e-06
CHUNKS = (0.5, 0.5)
TAIL = 16
MIB = 1 << 20

F32 = jnp.float32
BF16 = jnp.bfloat16
I32 = jnp.int32


def shifted(value, axis, steps):
    count = lax.axis_size(axis)
    first, last = (max(0, -steps), min(count, count - steps))
    return lax.ppermute(value, axis, [(source, source + steps) for source in range(first, last)])


def rotated(value, axis, steps):
    count = lax.axis_size(axis)
    return lax.ppermute(value, axis, [(source, (source + steps) % count) for source in range(count)])


def rms_norm(values, gain):
    return values * lax.rsqrt(jnp.mean(values * values, axis=-1, keepdims=True) + NORM_EPS) * gain


def half_silu(half):
    return half + half * jnp.tanh(half)


VMEM_SPEC = pl.BlockSpec(memory_space=pltpu.VMEM)
SMEM_SPEC = pl.BlockSpec(memory_space=pltpu.SMEM)


def cost(flops, nbytes):
    return pl.CostEstimate(flops=int(flops), bytes_accessed=int(nbytes), transcendentals=0)


def limit(mib):
    return pltpu.CompilerParams(vmem_limit_bytes=mib * MIB)


def make_weights(model_width, width):
    def kernel(me, w_q, w_k, w_v, out):
        queries = w_q[...]
        low = lax.broadcasted_iota(I32, queries.shape, 1) < HEAD_DIM
        zero = jnp.zeros_like(queries)
        out[:, :width] = jnp.where(low, queries, zero)
        out[:, width : 2 * width] = jnp.where(low, zero, queries)
        out[:, 2 * width : 3 * width] = w_k[...]
        out[:, 3 * width :] = w_v[...]

    per = model_width // width
    block = lambda index: pl.BlockSpec(
        (model_width, width), lambda i, me: (0, index * per + me[0])
    )
    return pl.pallas_call(
        kernel,
        grid_spec=pltpu.PrefetchScalarGridSpec(
            num_scalar_prefetch=1,
            grid=(1,),
            in_specs=[block(1), block(2), block(3)],
            out_specs=pl.BlockSpec((model_width, 4 * width), lambda i, me: (0, 0)),
        ),
        out_shape=jax.ShapeDtypeStruct((model_width, 4 * width), BF16),
        compiler_params=limit(4),
        cost_estimate=cost(0, 16 * model_width * width),
        name="weights",
    )


def make_project(group, blocks, block_rows, width, model_width):
    lane = model_width // group
    first, past = blocks
    per = past - first
    rows = per * block_rows
    opening = first == 0

    def kernel(me_ref, *refs):
        refs = list(refs)
        take = lambda number: [refs.pop(0) for _ in range(number)]
        known = None if opening else take(1)[0]
        pieces = take(group)
        gains, weights = take(2)
        q_ref, kv_ref, emb_ref = take(3)
        lives_ref = take(1)[0] if opening else None
        me = me_ref[0]
        offsets = (0, group - 1, 1, 2)
        for piece, offset in zip(pieces, offsets):
            column = lax.rem(me + offset, group)
            emb_ref[:, pl.ds(pl.multiple_of(column * lane, lane), lane)] = piece[pl.ds(0, rows), :]
            if opening:
                code = piece[rows : rows + TAIL, :].astype(F32)
                high, low = (jnp.max(code[at : at + 1]) for at in (TAIL - 2, TAIL - 1))
                lives_ref[column] = (high * TAIL + low).astype(I32)
        lives = [(lives_ref if opening else known)[b] for b in range(group)]
        for part in range(per):
            here = pl.ds(part * block_rows, block_rows)
            position = lax.broadcasted_iota(I32, (block_rows, 1), 0)
            mask = (position < lives[first + part]).astype(F32)
            embedded = emb_ref[here, :].astype(F32)
            normed = (rms_norm(embedded, gains[0:1, :]) * mask).astype(BF16)
            projected = jnp.dot(normed, weights[...], preferred_element_type=F32)
            scale = 0.5 / math.sqrt(HEAD_DIM)
            q_ref[here, :] = projected[:, : 2 * width].astype(BF16) * jnp.asarray(scale, BF16)
            kv_ref[here, :] = projected[:, 2 * width :].astype(BF16)
        if opening:
            row = lax.broadcasted_iota(I32, (TAIL, 2 * width), 0)
            code = jnp.zeros((TAIL, 2 * width), F32)
            for b in range(group):
                high = lax.div(lives[b], TAIL)
                code = jnp.where(row == b, high.astype(F32), code)
                code = jnp.where(row == group + b, (lives[b] - high * TAIL).astype(F32), code)
            kv_ref[pl.ds(rows, TAIL), :] = code.astype(BF16)

    more = TAIL if opening else 0
    out_shape = (
        jax.ShapeDtypeStruct((rows, 2 * width), BF16),
        jax.ShapeDtypeStruct((rows + more, 2 * width), BF16),
        jax.ShapeDtypeStruct((rows, model_width), BF16),
    )
    out_specs = (VMEM_SPEC,) * 3
    if opening:
        out_shape += (jax.ShapeDtypeStruct((group,), I32),)
        out_specs += (SMEM_SPEC,)
    return pl.pallas_call(
        kernel,
        out_shape=out_shape,
        in_specs=[SMEM_SPEC] * (1 if opening else 2) + [VMEM_SPEC] * (group + 2),
        out_specs=out_specs,
        compiler_params=limit(16),
        cost_estimate=cost(2 * rows * model_width * 4 * width, 4 * rows * model_width),
    )


def pair(queries, q_at, q_pos, kv_ref, k_at, k_pos, acc_ref, acc_at, rows, keep, live, tile_keys, width):
    tiles = lax.div(live + (tile_keys - 1), tile_keys)

    def step(tile, carry):
        at = pl.ds(pl.multiple_of(k_at + tile * tile_keys, tile_keys), tile_keys)
        keys = kv_ref[at, :width]
        values = kv_ref[at, width:]
        low = lax.broadcasted_iota(I32, values.shape, 1) < HEAD_DIM
        zero = jnp.zeros_like(values)
        total = None
        for head in range(2):
            half = lax.dot_general(
                queries[pl.ds(q_at, rows), head * width : (head + 1) * width],
                keys,
                (((1,), (1,)), ((), ())),
                preferred_element_type=F32,
            )
            weights = half_silu(half)
            if keep is not None:
                query = lax.broadcasted_iota(I32, weights.shape, 0) + q_pos
                key = lax.broadcasted_iota(I32, weights.shape, 1) + (k_pos + tile * tile_keys)
                weights = jnp.where(keep(query, key), weights, 0.0)
            held = jnp.where(low, values, zero) if head == 0 else jnp.where(low, zero, values)
            term = jnp.dot(weights.astype(BF16), held, preferred_element_type=F32)
            total = term if total is None else total + term
        acc_ref[pl.ds(acc_at, rows), :] += total
        return carry

    lax.fori_loop(0, tiles, step, 0)


def from_before(query, key):
    return key >= query


def from_after(query, key):
    return key <= query


def read_lives(kv_ref, rows, group):
    code = kv_ref[pl.ds(rows, TAIL), :].astype(F32)
    return [
        (jnp.max(code[b : b + 1]) * TAIL + jnp.max(code[group + b : group + b + 1])).astype(I32)
        for b in range(group)
    ]


def spans(first, past, chunks):
    for index, (start, end) in enumerate(chunks):
        low, high = max(first, start), min(past, end)
        if low < high:
            yield index, low, high


def make_own(chunks, opening, block_rows, width):
    group = chunks[-1][1]
    first_end = chunks[-1][0]
    parts = chunks[:-1] if opening else [(0, first_end), chunks[-1]]
    blocks = first_end if opening else group
    done = 0 if opening else first_end * block_rows
    total = blocks * block_rows

    def kernel(lives_ref, *refs):
        refs = list(refs)
        take = lambda number: [refs.pop(0) for _ in range(number)]
        queries = take(len(parts))
        keys = take(len(chunks) - 1 if opening else len(chunks))
        old = None if opening else take(1)[0]
        acc, q_all = take(2)
        if not opening:
            acc[pl.ds(0, done), :] = old[...]
        acc[pl.ds(done, total - done), :] = jnp.zeros((total - done, width), F32)
        for (low, high), ref in zip(parts, queries):
            q_all[pl.ds(low * block_rows, (high - low) * block_rows), :] = ref[...]
        for k in range(blocks):
            home = next(spans(k, k + 1, chunks))[0]
            start = 0 if opening or k >= first_end else first_end
            while start < blocks:
                past = min(start + 2, blocks)
                pair(
                    q_all,
                    start * block_rows,
                    start * block_rows,
                    keys[home],
                    (k - chunks[home][0]) * block_rows,
                    k * block_rows,
                    acc,
                    start * block_rows,
                    (past - start) * block_rows,
                    None,
                    lives_ref[k],
                    block_rows,
                    width,
                )
                start = past

    inputs = len(parts) + (len(chunks) - 1 if opening else len(chunks) + 1)
    pairs = first_end**2 if opening else group**2 - first_end**2
    return pl.pallas_call(
        kernel,
        out_shape=(
            jax.ShapeDtypeStruct((total, width), F32),
            jax.ShapeDtypeStruct((total, 2 * width), BF16),
        ),
        in_specs=[SMEM_SPEC] + [VMEM_SPEC] * inputs,
        out_specs=(VMEM_SPEC,) * 2,
        compiler_params=limit(24),
        cost_estimate=cost(pairs * block_rows**2 * 2048, total * width * 8),
        name="own0" if opening else "own1",
    )


def make_near(c, chunks, block_rows, width):
    first, past = chunks[c]
    known = chunks[-1][0]
    head_rows = chunks[0][1] * block_rows

    def kernel(*refs):
        before, after = refs[:2]
        heads = refs[2:-3] or (before, after)
        queries, old, acc = refs[-3:]
        acc[...] = old[...]
        lives_before = read_lives(heads[0], head_rows, chunks[-1][1])
        lives_after = read_lives(heads[1], head_rows, chunks[-1][1])
        for k in range(first, past):
            jobs = [(before, 0, k, None), (before, k, k + 1, from_before)]
            jobs += [(after, k, k + 1, from_after), (after, k + 1, known, None)]
            for held, low, high, keep in jobs:
                if low == high:
                    continue
                pair(
                    queries,
                    low * block_rows,
                    low * block_rows,
                    held,
                    (k - first) * block_rows,
                    k * block_rows,
                    acc,
                    low * block_rows,
                    (high - low) * block_rows,
                    keep,
                    (lives_before if held is before else lives_after)[k],
                    block_rows // 2,
                    width,
                )

    operands = 4 if c == 0 else 6
    return pl.pallas_call(
        kernel,
        out_shape=jax.ShapeDtypeStruct((known * block_rows, width), F32),
        in_specs=[VMEM_SPEC] * operands,
        out_specs=VMEM_SPEC,
        input_output_aliases={operands - 1: 0},
        compiler_params=limit(20),
        cost_estimate=cost(3 * block_rows**2 * 2048, known * block_rows * width * 8),
    )


def make_last(batch, chunks, block_rows, width, capacity):
    count = len(chunks)
    first, blocks = chunks[-1]
    head_rows = chunks[0][1] * block_rows
    size = len(batch) * capacity

    def kernel(*refs):
        after = refs[:count]
        before, first_before = refs[count : count + 2]
        queries, old, slots = refs[count + 2 : count + 5]
        out = refs[count + 5 : -1]
        acc = refs[-1]
        lives_before = read_lives(first_before, head_rows, blocks)
        lives_after = read_lives(after[0], head_rows, blocks)
        for order, q in enumerate(batch):
            at = q * block_rows
            acc[...] = old[pl.ds(at, block_rows), :]

            def run(held, k, keep, live):
                start = chunks[next(spans(k, k + 1, chunks))[0]][0]
                pair(
                    queries,
                    at,
                    at,
                    held,
                    (k - start) * block_rows,
                    k * block_rows,
                    acc,
                    0,
                    block_rows,
                    keep,
                    live,
                    block_rows // 2,
                    width,
                )

            for k in range(blocks):
                home = next(spans(k, k + 1, chunks))[0]
                if k >= first and q <= k:
                    run(before, k, from_before if q == k else None, lives_before[k])
                if q >= first and q >= k:
                    run(after[home], k, from_after if q == k else None, lives_after[k])
            attended = acc[...].astype(BF16)
            for turn in range(blocks):
                place = lax.broadcasted_iota(I32, (capacity, block_rows), 0) + turn * capacity
                pick = jnp.where(place == slots[q : q + 1, :], 1.0, 0.0).astype(BF16)
                out[turn][pl.ds(order * capacity, capacity), :] = jnp.dot(
                    pick, attended, preferred_element_type=F32
                ).astype(BF16)

    return pl.pallas_call(
        kernel,
        out_shape=(jax.ShapeDtypeStruct((size, width), BF16),) * blocks,
        in_specs=[VMEM_SPEC] * (count + 5),
        out_specs=(VMEM_SPEC,) * blocks,
        scratch_shapes=[pltpu.VMEM((block_rows, width), F32)],
        compiler_params=limit(20),
        cost_estimate=cost(7 * block_rows**2 * 2048, block_rows * width * 16),
    )


def make_slots(group, head_rows, block_rows, capacity):
    lanes = 128
    strips = block_rows // lanes

    def kernel(me_ref, lives_ref, *refs):
        pieces = refs[:group]
        slots, slot_col = refs[group:]
        me = me_ref[0]
        earlier = lax.broadcasted_iota(I32, (block_rows, block_rows), 0) < lax.broadcasted_iota(
            I32, (block_rows, block_rows), 1
        )
        earlier = jnp.where(earlier, 1.0, 0.0).astype(BF16)
        position = lax.broadcasted_iota(I32, (1, block_rows), 1)
        expert = lax.broadcasted_iota(I32, (8, block_rows), 0)
        for piece, offset in zip(pieces, (0, group - 1, 1, 2)):
            block = lax.rem(me + offset, group)
            code = piece[pl.ds(head_rows, TAIL), :].astype(F32)
            domain = jnp.concatenate([code[r : r + 1, :] for r in range(strips)], axis=1)
            turn = domain.astype(I32) - me
            turn = jnp.where(turn < 0, turn + group, turn)
            alive = position < lives_ref[block]
            onehot = jnp.where((expert == turn) & alive, 1.0, 0.0)
            rank = jnp.dot(onehot.astype(BF16), earlier, preferred_element_type=F32)
            slot = jnp.sum(
                onehot * (rank + (expert * capacity).astype(F32)), axis=0, keepdims=True
            )
            slot = jnp.where(alive, slot, -1.0)
            slots[pl.ds(block, 1), :] = slot.astype(I32)
            if offset == 0:
                slot_col[...] = jnp.transpose(jnp.broadcast_to(slot, (lanes, block_rows))).astype(
                    I32
                )

    return pl.pallas_call(
        kernel,
        out_shape=(
            jax.ShapeDtypeStruct((8, block_rows), I32),
            jax.ShapeDtypeStruct((block_rows, lanes), I32),
        ),
        in_specs=[SMEM_SPEC] * 2 + [VMEM_SPEC] * group,
        out_specs=(VMEM_SPEC,) * 2,
        compiler_params=limit(12),
        cost_estimate=cost(2 * 32 * block_rows**2, 8 * block_rows * lanes),
        name="slots",
    )


def make_select(batch, chunks, block_rows, model_width, capacity):
    homes = [next(spans(b, b + 1, chunks))[0] for b in batch]
    size = len(batch) * capacity

    def kernel(*refs):
        sources = refs[: len(batch)]
        slots, gains, weights, emb, gating = refs[len(batch) :]
        for order, (b, home, source) in enumerate(zip(batch, homes, sources)):
            place = lax.broadcasted_iota(I32, (capacity, block_rows), 0)
            pick = jnp.where(place == slots[b : b + 1, :], 1.0, 0.0).astype(BF16)
            rows = source[pl.ds((b - chunks[home][0]) * block_rows, block_rows), :]
            emb[pl.ds(order * capacity, capacity), :] = jnp.dot(
                pick, rows, preferred_element_type=F32
            ).astype(BF16)
        normed = rms_norm(emb[...].astype(F32), gains[0:1, :]).astype(BF16)
        gate = jnp.dot(normed, weights[...], preferred_element_type=F32)
        gating[...] = half_silu(gate * 0.5)

    return homes, pl.pallas_call(
        kernel,
        grid=(1,),
        out_shape=(
            jax.ShapeDtypeStruct((size, model_width), BF16),
            jax.ShapeDtypeStruct((size, model_width), F32),
        ),
        in_specs=[VMEM_SPEC] * (len(batch) + 2)
        + [pl.BlockSpec((model_width, model_width), lambda i: (0, 0))],
        out_specs=(VMEM_SPEC,) * 2,
        compiler_params=limit(12),
        cost_estimate=cost(4 * size * model_width**2, 8 * size * model_width),
    )


def make_serve(batch, senders, group, width, model_width, hidden_units, capacity):
    size = len(batch) * capacity
    tile = hidden_units // 4

    def kernel(me_ref, *refs):
        pieces = refs[:group]
        emb, gating, gains, proj_out, w_in, w_out = refs[group : group + 6]
        out = refs[group + 6 : -2]
        att, done = refs[-2:]
        me = me_ref[0]
        for k, piece in enumerate(pieces):
            column = lax.rem(me + group - k, group)
            att[:, pl.ds(pl.multiple_of(column * width, width), width)] = piece[...].astype(F32)
        gated = (rms_norm(att[...], gains[1:2, :]) * gating[...]).astype(BF16)
        hidden = emb[...].astype(F32) + jnp.dot(
            gated, proj_out[...], preferred_element_type=F32
        )
        routed = rms_norm(hidden, gains[2:3, :]).astype(BF16)
        total = None
        for at in range(0, hidden_units, tile):
            gate = jnp.dot(routed, w_in[0, :, at : at + tile], preferred_element_type=F32)
            up = jnp.dot(
                routed,
                w_in[0, :, hidden_units + at : hidden_units + at + tile],
                preferred_element_type=F32,
            )
            activated = (half_silu(gate * 0.5) * up).astype(BF16)
            term = jnp.dot(activated, w_out[0, at : at + tile, :], preferred_element_type=F32)
            total = term if total is None else total + term
        done[...] = (hidden + total.astype(BF16).astype(F32)).astype(BF16)
        for ref, sender in zip(out, (*senders, batch[0])):
            at = jnp.where(me == sender, 0, capacity)
            ref[...] = done[pl.ds(pl.multiple_of(at, capacity), capacity), :]

    return pl.pallas_call(
        kernel,
        out_shape=(jax.ShapeDtypeStruct((capacity, model_width), BF16),) * (len(senders) + 1),
        in_specs=[SMEM_SPEC] + [VMEM_SPEC] * (group + 6),
        out_specs=(VMEM_SPEC,) * (len(senders) + 1),
        scratch_shapes=[
            pltpu.VMEM((size, model_width), F32),
            pltpu.VMEM((size, model_width), BF16),
        ],
        compiler_params=limit(20),
        cost_estimate=cost(6 * size * model_width * hidden_units, 8 * size * model_width),
    )


def make_mix(group, exchanges, rows, model_width, capacity):
    def kernel(me_ref, *refs):
        pieces, (slot, out) = refs[:-2], refs[-2:]
        me = me_ref[0]
        where = slot[:, 0:1]
        per = len(pieces) // 2
        first = functools.reduce(
            jnp.logical_or, [me == target for _, target in exchanges[0][0]]
        )
        total = None
        for j in range(per):
            piece = jnp.where(
                lax.broadcasted_iota(I32, (capacity, model_width), 0) * 0 + first.astype(I32) > 0,
                pieces[j][...].astype(F32),
                pieces[per + j][...].astype(F32),
            ).astype(BF16)
            turn = jnp.zeros_like(me)
            if j < per - 1:
                for exchange in exchanges:
                    for source, target in exchange[j]:
                        turn = jnp.where(me == target, (source - target) % group, turn)
            place = lax.broadcasted_iota(I32, (rows, capacity), 1) + turn * capacity
            pick = jnp.where(place == where, 1.0, 0.0).astype(BF16)
            term = jnp.dot(pick, piece, preferred_element_type=F32)
            total = term if total is None else total + term
        out[...] = total.astype(BF16)

    return pl.pallas_call(
        kernel,
        out_shape=jax.ShapeDtypeStruct((rows, model_width), BF16),
        in_specs=[SMEM_SPEC] + [VMEM_SPEC] * (2 * (len(exchanges[0]) + 1) + 1),
        out_specs=VMEM_SPEC,
        compiler_params=limit(16),
        cost_estimate=cost(4 * rows * rows * model_width, 8 * rows * model_width),
        name="mix",
    )


BATCHES = ((0, 3), (1, 2))
HOMEWARD = (
    (((1, 0), (2, 3)), ((2, 0), (1, 3)), ((3, 0), (0, 3))),
    (((0, 1), (3, 2)), ((2, 1), (1, 2)), ((3, 1), (0, 2))),
)


def by_heads(
    item_ids, domains, live_counts, table, norm_gains, proj_in, proj_out, expert_in, expert_out
):
    group = lax.axis_size("emb")
    me = lax.axis_index("emb").astype(I32)[None]
    rows = domains.shape[0]
    model_width = proj_out.shape[0]
    hidden_units = expert_out.shape[1]
    width = model_width // group
    capacity = 2 * rows // group
    ends = [round(group * sum(CHUNKS[: c + 1])) for c in range(len(CHUNKS))]
    chunks = list(zip([0, *ends[:-1]], ends))

    high = lax.div(live_counts[0], TAIL)
    count_code = jnp.stack((high, live_counts[0] - high * TAIL))
    code = jnp.concatenate(
        (
            domains.reshape(rows // width, width),
            jnp.zeros((TAIL - 2 - rows // width, width), I32),
            jnp.broadcast_to(count_code[:, None], (2, width)),
        )
    ).astype(BF16)
    cut = chunks[0][1] * rows
    fetch = lambda ids: table.at[ids].get(mode="promise_in_bounds", wrap_negative_indices=False)
    opening = jnp.concatenate((fetch(item_ids[:cut]), code))
    rest = fetch(item_ids[cut:])
    mine = [opening] + [rest[a * rows - cut : b * rows - cut] for a, b in chunks[1:]]
    low, high, far = [], [], []
    for c, piece in enumerate(mine):
        low.append(rotated(piece, "emb", 1))
        high.append(rotated(piece, "emb", -1))
        far.append(rotated(low[c], "emb", 1))

    weights = make_weights(model_width, width)(me, proj_in, proj_in, proj_in)
    queries, own, before, after, embedded = [], [], [], [], []
    lives = acc = None
    for c, blocks in enumerate(chunks):
        project = make_project(group, blocks, rows, width, model_width)
        known = () if c == 0 else (lives,)
        pieces = (mine[c], low[c], high[c], far[c])
        q, kv, emb, *more = project(me, *known, *pieces, norm_gains, weights)
        if c == 0:
            lives = more[0]
            slots, slot_col = make_slots(group, cut, rows, capacity)(me, lives, *pieces)
        queries.append(q)
        own.append(kv)
        embedded.append(emb)
        before.append(shifted(kv, "seq", 1))
        after.append(shifted(kv, "seq", -1))
        if c == len(chunks) - 2:
            acc, q_all = make_own(chunks, True, rows, width)(lives, *queries, *own)
    for c in range(len(chunks) - 1):
        heads = () if c == 0 else (before[0], after[0])
        acc = make_near(c, chunks, rows, width)(before[c], after[c], *heads, q_all, acc)
    acc, q_all = make_own(chunks, False, rows, width)(lives, q_all, queries[-1], *own, acc)

    sent = []
    for batch in BATCHES:
        last = make_last(batch, chunks, rows, width, capacity)
        shares = last(*after, before[-1], before[0], q_all, acc, slots)
        arrived = [shares[0]]
        for k in range(1, group):
            arrived.append(rotated(shares[k], "emb", k))
        sent.append(arrived)
    finished = []
    for n, batch in enumerate(BATCHES):
        homes, select = make_select(batch, chunks, rows, model_width, capacity)
        emb, gating = select(*(embedded[h] for h in homes), slots, norm_gains, proj_in)
        senders = [source for pairs in HOMEWARD[n] for source, target in pairs[:1]]
        serve = make_serve(batch, senders, group, width, model_width, hidden_units, capacity)
        made = serve(
            me, *sent[n], emb, gating, norm_gains, proj_out, expert_in, expert_out
        )
        for j, pairs in enumerate(HOMEWARD[n]):
            finished.append(lax.ppermute(made[j], "emb", pairs))
        finished.append(made[-1])
    mix = make_mix(group, HOMEWARD, rows, model_width, capacity)
    return mix(me, *finished, slot_col)


def by_rows(
    item_ids, domains, live_counts, table, norm_gains, proj_in, proj_out, expert_in, expert_out
):
    rows_dev = domains.shape[0]
    model_width = proj_out.shape[0]
    hidden_units = expert_out.shape[1]
    group_size = lax.axis_size("emb")
    capacity = 2 * rows_dev // group_size
    columns = table[item_ids]
    embedded = lax.all_to_all(columns, "emb", split_axis=0, concat_axis=1, tiled=True).astype(
        jnp.float32
    )
    positions = jnp.arange(rows_dev, dtype=jnp.int32)
    live_mask = (positions < live_counts[0]).astype(jnp.float32)
    normed = (rms_norm(embedded, norm_gains[0]) * live_mask[:, None]).astype(jnp.bfloat16)
    projected = jnp.dot(normed, proj_in, preferred_element_type=jnp.float32)
    gating = jax.nn.silu(projected[:, :model_width])
    queries = (
        projected[:, model_width : 2 * model_width]
        .astype(jnp.bfloat16)
        .reshape(rows_dev, HEADS, HEAD_DIM)
    )
    own_pair = jnp.stack(
        (
            projected[:, 2 * model_width : 3 * model_width].astype(jnp.bfloat16),
            projected[:, 3 * model_width :].astype(jnp.bfloat16),
        )
    )
    key_weights = proj_in[:, 2 * model_width :]
    upper_band = positions[None, :] >= positions[:, None]
    lower_band = positions[None, :] <= positions[:, None]
    score_scale = 1.0 / math.sqrt(HEAD_DIM)

    def unpack(piece):
        rebuilt = jnp.dot(piece[0], key_weights, preferred_element_type=jnp.float32)
        return jnp.stack(
            (
                rebuilt[:, :model_width].astype(jnp.bfloat16),
                rebuilt[:, model_width:].astype(jnp.bfloat16),
            )
        )

    def attend(both, band_mask):
        key_heads = both[0].reshape(rows_dev, HEADS, HEAD_DIM)
        value_heads = both[1].reshape(rows_dev, HEADS, HEAD_DIM)
        scores = (
            jnp.einsum("qhd,khd->hqk", queries, key_heads, preferred_element_type=jnp.float32)
            * score_scale
        )
        weights = jax.nn.silu(scores)
        if band_mask is not None:
            weights = jnp.where(band_mask[None], weights, 0.0)
        weights = weights.astype(jnp.bfloat16)
        return jnp.einsum(
            "hqk,khd->qhd", weights, value_heads, preferred_element_type=jnp.float32
        ).reshape(rows_dev, model_width)

    outgoing = normed[None]
    attended = attend(own_pair, None)
    for distance in range(1, SPAN + 1):
        band_before = upper_band if distance == SPAN else None
        band_after = lower_band if distance == SPAN else None
        earlier = shifted(outgoing, ("seq", "emb"), distance)
        following = shifted(outgoing, ("seq", "emb"), -distance)
        attended = (
            attended + attend(unpack(earlier), band_before) + attend(unpack(following), band_after)
        )
    gated = (rms_norm(attended, norm_gains[1]) * gating).astype(jnp.bfloat16)
    hidden = embedded + jnp.dot(gated, proj_out, preferred_element_type=jnp.float32)
    routed = rms_norm(hidden, norm_gains[2]).astype(jnp.bfloat16)
    onehot_domain = (domains[:, None] == jnp.arange(group_size, dtype=jnp.int32)[None, :]).astype(
        jnp.int32
    )
    slot_rank = jnp.sum((jnp.cumsum(onehot_domain, axis=0) - onehot_domain) * onehot_domain, axis=1)
    slot_index = domains * capacity + slot_rank
    outgoing_rows = (
        jnp.zeros((group_size * capacity, model_width), jnp.bfloat16).at[slot_index].set(routed)
    )
    outgoing_rows = outgoing_rows.reshape(group_size, capacity, model_width)
    inbox = lax.all_to_all(outgoing_rows, "emb", split_axis=0, concat_axis=0, tiled=True)
    sources, slot_count, _ = inbox.shape
    flattened = inbox.reshape(sources * slot_count, model_width)
    gate_up = jnp.dot(flattened, expert_in[0], preferred_element_type=jnp.float32)
    activated = (jax.nn.silu(gate_up[:, :hidden_units]) * gate_up[:, hidden_units:]).astype(
        jnp.bfloat16
    )
    produced = jnp.dot(activated, expert_out[0], preferred_element_type=jnp.float32).astype(
        jnp.bfloat16
    )
    finished = produced.reshape(sources, slot_count, model_width)
    returned = lax.all_to_all(finished, "emb", split_axis=0, concat_axis=0, tiled=True).reshape(
        group_size * capacity, model_width
    )
    expert_rows = returned[slot_index].astype(jnp.float32)
    return (live_mask[:, None] * (hidden + expert_rows)).astype(jnp.bfloat16)


def solution(mesh):
    group = mesh.shape["emb"]
    split_heads = group == SPAN and HEADS == 2 * group

    def body(*arrays):
        return (by_heads if split_heads else by_rows)(*arrays)

    in_specs = (
        P("seq"),
        P(("seq", "emb")),
        P(("seq", "emb")),
        P(None, "emb"),
        P(),
        P(),
        P(),
        P("emb", None, None),
        P("emb", None, None),
    )
    out_specs = P(("seq", "emb"), None)
    return jax.shard_map(body, mesh=mesh, in_specs=in_specs, out_specs=out_specs, check_vma=False)
```

```python
import functools
import math

import jax
import jax.numpy as jnp
from jax import lax
from jax.experimental import pallas as pl
from jax.experimental.pallas import tpu as pltpu
from jax.sharding import PartitionSpec as P


HEADS = 8
HEAD_DIM = 64
SPAN = 4
NORM_EPS = 1e-06
CHUNKS = (0.5, 0.5)
TAIL = 16
MIB = 1 << 20

F32 = jnp.float32
BF16 = jnp.bfloat16
I32 = jnp.int32


def shifted(value, axis, steps):
    count = lax.axis_size(axis)
    first, last = (max(0, -steps), min(count, count - steps))
    return lax.ppermute(value, axis, [(source, source + steps) for source in range(first, last)])


def rotated(value, axis, steps):
    count = lax.axis_size(axis)
    return lax.ppermute(value, axis, [(source, (source + steps) % count) for source in range(count)])


def rms_norm(values, gain):
    return values * lax.rsqrt(jnp.mean(values * values, axis=-1, keepdims=True) + NORM_EPS) * gain


def half_silu(half):
    return half + half * jnp.tanh(half)


VMEM_SPEC = pl.BlockSpec(memory_space=pltpu.VMEM)
SMEM_SPEC = pl.BlockSpec(memory_space=pltpu.SMEM)


def cost(flops, nbytes):
    return pl.CostEstimate(flops=int(flops), bytes_accessed=int(nbytes), transcendentals=0)


def limit(mib):
    return pltpu.CompilerParams(vmem_limit_bytes=mib * MIB)


def make_weights(model_width, width):
    def kernel(me, w_q, w_k, w_v, out):
        queries = w_q[...]
        low = lax.broadcasted_iota(I32, queries.shape, 1) < HEAD_DIM
        zero = jnp.zeros_like(queries)
        out[:, :width] = jnp.where(low, queries, zero)
        out[:, width : 2 * width] = jnp.where(low, zero, queries)
        out[:, 2 * width : 3 * width] = w_k[...]
        out[:, 3 * width :] = w_v[...]

    per = model_width // width
    block = lambda index: pl.BlockSpec(
        (model_width, width), lambda i, me: (0, index * per + me[0])
    )
    return pl.pallas_call(
        kernel,
        grid_spec=pltpu.PrefetchScalarGridSpec(
            num_scalar_prefetch=1,
            grid=(1,),
            in_specs=[block(1), block(2), block(3)],
            out_specs=pl.BlockSpec((model_width, 4 * width), lambda i, me: (0, 0)),
        ),
        out_shape=jax.ShapeDtypeStruct((model_width, 4 * width), BF16),
        compiler_params=limit(4),
        cost_estimate=cost(0, 16 * model_width * width),
        name="weights",
    )


def make_project(group, blocks, block_rows, width, model_width):
    lane = model_width // group
    first, past = blocks
    per = past - first
    rows = per * block_rows
    opening = first == 0

    def kernel(me_ref, *refs):
        refs = list(refs)
        take = lambda number: [refs.pop(0) for _ in range(number)]
        known = None if opening else take(1)[0]
        pieces = take(group)
        gains, weights = take(2)
        q_ref, kv_ref, emb_ref = take(3)
        lives_ref = take(1)[0] if opening else None
        me = me_ref[0]
        offsets = (0, group - 1, 1, 2)
        for piece, offset in zip(pieces, offsets):
            column = lax.rem(me + offset, group)
            emb_ref[:, pl.ds(pl.multiple_of(column * lane, lane), lane)] = piece[pl.ds(0, rows), :]
            if opening:
                code = piece[rows : rows + TAIL, :].astype(F32)
                high, low = (jnp.max(code[at : at + 1]) for at in (TAIL - 2, TAIL - 1))
                lives_ref[column] = (high * TAIL + low).astype(I32)
        lives = [(lives_ref if opening else known)[b] for b in range(group)]
        for part in range(per):
            here = pl.ds(part * block_rows, block_rows)
            position = lax.broadcasted_iota(I32, (block_rows, 1), 0)
            mask = (position < lives[first + part]).astype(F32)
            embedded = emb_ref[here, :].astype(F32)
            normed = (rms_norm(embedded, gains[0:1, :]) * mask).astype(BF16)
            projected = jnp.dot(normed, weights[...], preferred_element_type=F32)
            scale = 0.5 / math.sqrt(HEAD_DIM)
            q_ref[here, :] = projected[:, : 2 * width].astype(BF16) * jnp.asarray(scale, BF16)
            kv_ref[here, :] = projected[:, 2 * width :].astype(BF16)
        if opening:
            row = lax.broadcasted_iota(I32, (TAIL, 2 * width), 0)
            code = jnp.zeros((TAIL, 2 * width), F32)
            for b in range(group):
                high = lax.div(lives[b], TAIL)
                code = jnp.where(row == b, high.astype(F32), code)
                code = jnp.where(row == group + b, (lives[b] - high * TAIL).astype(F32), code)
            kv_ref[pl.ds(rows, TAIL), :] = code.astype(BF16)

    more = TAIL if opening else 0
    out_shape = (
        jax.ShapeDtypeStruct((rows, 2 * width), BF16),
        jax.ShapeDtypeStruct((rows + more, 2 * width), BF16),
        jax.ShapeDtypeStruct((rows, model_width), BF16),
    )
    out_specs = (VMEM_SPEC,) * 3
    if opening:
        out_shape += (jax.ShapeDtypeStruct((group,), I32),)
        out_specs += (SMEM_SPEC,)
    return pl.pallas_call(
        kernel,
        out_shape=out_shape,
        in_specs=[SMEM_SPEC] * (1 if opening else 2) + [VMEM_SPEC] * (group + 2),
        out_specs=out_specs,
        compiler_params=limit(16),
        cost_estimate=cost(2 * rows * model_width * 4 * width, 4 * rows * model_width),
    )


def pair(queries, q_at, q_pos, kv_ref, k_at, k_pos, acc_ref, acc_at, rows, keep, live, tile_keys, width):
    tiles = lax.div(live + (tile_keys - 1), tile_keys)

    def step(tile, carry):
        at = pl.ds(pl.multiple_of(k_at + tile * tile_keys, tile_keys), tile_keys)
        keys = kv_ref[at, :width]
        values = kv_ref[at, width:]
        low = lax.broadcasted_iota(I32, values.shape, 1) < HEAD_DIM
        zero = jnp.zeros_like(values)
        total = None
        for head in range(2):
            half = lax.dot_general(
                queries[pl.ds(q_at, rows), head * width : (head + 1) * width],
                keys,
                (((1,), (1,)), ((), ())),
                preferred_element_type=F32,
            )
            weights = half_silu(half)
            if keep is not None:
                query = lax.broadcasted_iota(I32, weights.shape, 0) + q_pos
                key = lax.broadcasted_iota(I32, weights.shape, 1) + (k_pos + tile * tile_keys)
                weights = jnp.where(keep(query, key), weights, 0.0)
            held = jnp.where(low, values, zero) if head == 0 else jnp.where(low, zero, values)
            term = jnp.dot(weights.astype(BF16), held, preferred_element_type=F32)
            total = term if total is None else total + term
        acc_ref[pl.ds(acc_at, rows), :] += total
        return carry

    lax.fori_loop(0, tiles, step, 0)


def from_before(query, key):
    return key >= query


def from_after(query, key):
    return key <= query


def read_lives(kv_ref, rows, group):
    code = kv_ref[pl.ds(rows, TAIL), :].astype(F32)
    return [
        (jnp.max(code[b : b + 1]) * TAIL + jnp.max(code[group + b : group + b + 1])).astype(I32)
        for b in range(group)
    ]


def spans(first, past, chunks):
    for index, (start, end) in enumerate(chunks):
        low, high = max(first, start), min(past, end)
        if low < high:
            yield index, low, high


def make_own(chunks, opening, block_rows, width):
    group = chunks[-1][1]
    first_end = chunks[-1][0]
    parts = chunks[:-1] if opening else [(0, first_end), chunks[-1]]
    blocks = first_end if opening else group
    done = 0 if opening else first_end * block_rows
    total = blocks * block_rows

    def kernel(lives_ref, *refs):
        refs = list(refs)
        take = lambda number: [refs.pop(0) for _ in range(number)]
        queries = take(len(parts))
        keys = take(len(chunks) - 1 if opening else len(chunks))
        old = None if opening else take(1)[0]
        acc, q_all = take(2)
        if not opening:
            acc[pl.ds(0, done), :] = old[...]
        acc[pl.ds(done, total - done), :] = jnp.zeros((total - done, width), F32)
        for (low, high), ref in zip(parts, queries):
            q_all[pl.ds(low * block_rows, (high - low) * block_rows), :] = ref[...]
        span = 2
        for home, (low, high) in enumerate(chunks[: len(keys)]):
            start = 0 if opening or low >= first_end else first_end
            strides = (blocks - start) // span

            def step(job, carry):
                k = low + lax.div(job, strides)
                at = (start + lax.rem(job, strides) * span) * block_rows
                at = pl.multiple_of(at, block_rows)
                pair(
                    q_all,
                    at,
                    at,
                    keys[home],
                    pl.multiple_of((k - low) * block_rows, block_rows),
                    k * block_rows,
                    acc,
                    at,
                    span * block_rows,
                    None,
                    lives_ref[k],
                    block_rows,
                    width,
                )
                return carry

            lax.fori_loop(0, (high - low) * strides, step, 0)

    inputs = len(parts) + (len(chunks) - 1 if opening else len(chunks) + 1)
    pairs = first_end**2 if opening else group**2 - first_end**2
    return pl.pallas_call(
        kernel,
        out_shape=(
            jax.ShapeDtypeStruct((total, width), F32),
            jax.ShapeDtypeStruct((total, 2 * width), BF16),
        ),
        in_specs=[SMEM_SPEC] + [VMEM_SPEC] * inputs,
        out_specs=(VMEM_SPEC,) * 2,
        compiler_params=limit(24),
        cost_estimate=cost(pairs * block_rows**2 * 2048, total * width * 8),
        name="own0" if opening else "own1",
    )


def make_near(c, chunks, block_rows, width):
    first, past = chunks[c]
    known = chunks[-1][0]
    head_rows = chunks[0][1] * block_rows

    def kernel(*refs):
        before, after = refs[:2]
        heads = refs[2:-3] or (before, after)
        queries, old, acc = refs[-3:]
        acc[...] = old[...]
        lives_before = read_lives(heads[0], head_rows, chunks[-1][1])
        lives_after = read_lives(heads[1], head_rows, chunks[-1][1])
        for k in range(first, past):
            jobs = [(before, 0, k, None), (before, k, k + 1, from_before)]
            jobs += [(after, k, k + 1, from_after), (after, k + 1, known, None)]
            for held, low, high, keep in jobs:
                if low == high:
                    continue
                pair(
                    queries,
                    low * block_rows,
                    low * block_rows,
                    held,
                    (k - first) * block_rows,
                    k * block_rows,
                    acc,
                    low * block_rows,
                    (high - low) * block_rows,
                    keep,
                    (lives_before if held is before else lives_after)[k],
                    block_rows // 2,
                    width,
                )

    operands = 4 if c == 0 else 6
    return pl.pallas_call(
        kernel,
        out_shape=jax.ShapeDtypeStruct((known * block_rows, width), F32),
        in_specs=[VMEM_SPEC] * operands,
        out_specs=VMEM_SPEC,
        input_output_aliases={operands - 1: 0},
        compiler_params=limit(20),
        cost_estimate=cost(3 * block_rows**2 * 2048, known * block_rows * width * 8),
    )


def make_last(batch, chunks, block_rows, width, capacity):
    count = len(chunks)
    first, blocks = chunks[-1]
    head_rows = chunks[0][1] * block_rows
    size = len(batch) * capacity

    def kernel(*refs):
        after = refs[:count]
        before, first_before = refs[count : count + 2]
        queries, old, slots = refs[count + 2 : count + 5]
        out = refs[count + 5 : -1]
        acc = refs[-1]
        lives_before = read_lives(first_before, head_rows, blocks)
        lives_after = read_lives(after[0], head_rows, blocks)
        for order, q in enumerate(batch):
            at = q * block_rows
            acc[...] = old[pl.ds(at, block_rows), :]

            def run(held, k, keep, live):
                start = chunks[next(spans(k, k + 1, chunks))[0]][0]
                pair(
                    queries,
                    at,
                    at,
                    held,
                    (k - start) * block_rows,
                    k * block_rows,
                    acc,
                    0,
                    block_rows,
                    keep,
                    live,
                    block_rows // 2,
                    width,
                )

            for k in range(blocks):
                home = next(spans(k, k + 1, chunks))[0]
                if k >= first and q <= k:
                    run(before, k, from_before if q == k else None, lives_before[k])
                if q >= first and q >= k:
                    run(after[home], k, from_after if q == k else None, lives_after[k])
            attended = acc[...].astype(BF16)
            for turn in range(blocks):
                place = lax.broadcasted_iota(I32, (capacity, block_rows), 0) + turn * capacity
                pick = jnp.where(place == slots[q : q + 1, :], 1.0, 0.0).astype(BF16)
                out[turn][pl.ds(order * capacity, capacity), :] = jnp.dot(
                    pick, attended, preferred_element_type=F32
                ).astype(BF16)

    return pl.pallas_call(
        kernel,
        out_shape=(jax.ShapeDtypeStruct((size, width), BF16),) * blocks,
        in_specs=[VMEM_SPEC] * (count + 5),
        out_specs=(VMEM_SPEC,) * blocks,
        scratch_shapes=[pltpu.VMEM((block_rows, width), F32)],
        compiler_params=limit(20),
        cost_estimate=cost(7 * block_rows**2 * 2048, block_rows * width * 16),
    )


def make_slots(group, tail_at, block_rows, capacity):
    lanes = 128
    strips = block_rows // lanes

    def kernel(me_ref, lives_ref, *refs):
        pieces = refs[:group]
        slots, slot_col = refs[group:]
        me = me_ref[0]
        earlier = lax.broadcasted_iota(I32, (block_rows, block_rows), 0) < lax.broadcasted_iota(
            I32, (block_rows, block_rows), 1
        )
        earlier = jnp.where(earlier, 1.0, 0.0).astype(BF16)
        position = lax.broadcasted_iota(I32, (1, block_rows), 1)
        expert = lax.broadcasted_iota(I32, (8, block_rows), 0)
        onehots, alives = [], []
        order = [lax.rem(me + offset, group) for offset in (0, group - 1, 1, 2)]
        for piece, block in zip(pieces, order):
            code = piece[pl.ds(tail_at, TAIL), :].astype(F32)
            domain = jnp.concatenate([code[r : r + 1, :] for r in range(strips)], axis=1)
            turn = domain.astype(I32) - me
            turn = jnp.where(turn < 0, turn + group, turn)
            alives.append(position < lives_ref[block])
            onehots.append(jnp.where((expert == turn) & alives[-1], 1.0, 0.0))
        ranks = jnp.dot(
            jnp.concatenate(onehots).astype(BF16), earlier, preferred_element_type=F32
        )
        for n, block in enumerate(order):
            rank = ranks[8 * n : 8 * n + 8] + (expert * capacity).astype(F32)
            slot = jnp.sum(onehots[n] * rank, axis=0, keepdims=True)
            slot = jnp.where(alives[n], slot, -1.0)
            slots[pl.ds(block, 1), :] = slot.astype(I32)
            if n == 0:
                slot_col[...] = jnp.transpose(jnp.broadcast_to(slot, (lanes, block_rows))).astype(
                    I32
                )

    return pl.pallas_call(
        kernel,
        out_shape=(
            jax.ShapeDtypeStruct((8, block_rows), I32),
            jax.ShapeDtypeStruct((block_rows, lanes), I32),
        ),
        in_specs=[SMEM_SPEC] * 2 + [VMEM_SPEC] * group,
        out_specs=(VMEM_SPEC,) * 2,
        compiler_params=limit(12),
        cost_estimate=cost(2 * 32 * block_rows**2, 8 * block_rows * lanes),
        name="slots",
    )


def make_select(batch, chunks, block_rows, model_width, capacity):
    homes = [next(spans(b, b + 1, chunks))[0] for b in batch]
    size = len(batch) * capacity

    def kernel(*refs):
        sources = refs[: len(batch)]
        slots, gains, weights, emb, gating = refs[len(batch) :]
        for order, (b, home, source) in enumerate(zip(batch, homes, sources)):
            place = lax.broadcasted_iota(I32, (capacity, block_rows), 0)
            pick = jnp.where(place == slots[b : b + 1, :], 1.0, 0.0).astype(BF16)
            rows = source[pl.ds((b - chunks[home][0]) * block_rows, block_rows), :]
            emb[pl.ds(order * capacity, capacity), :] = jnp.dot(
                pick, rows, preferred_element_type=F32
            ).astype(BF16)
        normed = rms_norm(emb[...].astype(F32), gains[0:1, :]).astype(BF16)
        gate = jnp.dot(normed, weights[...], preferred_element_type=F32)
        gating[...] = half_silu(gate * 0.5)

    return homes, pl.pallas_call(
        kernel,
        grid=(1,),
        out_shape=(
            jax.ShapeDtypeStruct((size, model_width), BF16),
            jax.ShapeDtypeStruct((size, model_width), F32),
        ),
        in_specs=[VMEM_SPEC] * (len(batch) + 2)
        + [pl.BlockSpec((model_width, model_width), lambda i: (0, 0))],
        out_specs=(VMEM_SPEC,) * 2,
        compiler_params=limit(12),
        cost_estimate=cost(4 * size * model_width**2, 8 * size * model_width),
    )


def make_serve(batch, senders, group, width, model_width, hidden_units, capacity):
    size = len(batch) * capacity
    tile = hidden_units // 4

    def kernel(me_ref, *refs):
        pieces = refs[:group]
        emb, gating, gains, proj_out, w_in, w_out = refs[group : group + 6]
        out = refs[group + 6 : -2]
        att, done = refs[-2:]
        me = me_ref[0]
        for k, piece in enumerate(pieces):
            column = lax.rem(me + group - k, group)
            att[:, pl.ds(pl.multiple_of(column * width, width), width)] = piece[...].astype(F32)
        gated = (rms_norm(att[...], gains[1:2, :]) * gating[...]).astype(BF16)
        hidden = emb[...].astype(F32) + jnp.dot(
            gated, proj_out[...], preferred_element_type=F32
        )
        routed = rms_norm(hidden, gains[2:3, :]).astype(BF16)
        total = None
        for at in range(0, hidden_units, tile):
            gate = jnp.dot(routed, w_in[0, :, at : at + tile], preferred_element_type=F32)
            up = jnp.dot(
                routed,
                w_in[0, :, hidden_units + at : hidden_units + at + tile],
                preferred_element_type=F32,
            )
            activated = (half_silu(gate * 0.5) * up).astype(BF16)
            term = jnp.dot(activated, w_out[0, at : at + tile, :], preferred_element_type=F32)
            total = term if total is None else total + term
        done[...] = (hidden + total.astype(BF16).astype(F32)).astype(BF16)
        for ref, sender in zip(out, (*senders, batch[0])):
            at = jnp.where(me == sender, 0, capacity)
            ref[...] = done[pl.ds(pl.multiple_of(at, capacity), capacity), :]

    return pl.pallas_call(
        kernel,
        out_shape=(jax.ShapeDtypeStruct((capacity, model_width), BF16),) * (len(senders) + 1),
        in_specs=[SMEM_SPEC] + [VMEM_SPEC] * (group + 6),
        out_specs=(VMEM_SPEC,) * (len(senders) + 1),
        scratch_shapes=[
            pltpu.VMEM((size, model_width), F32),
            pltpu.VMEM((size, model_width), BF16),
        ],
        compiler_params=limit(20),
        cost_estimate=cost(6 * size * model_width * hidden_units, 8 * size * model_width),
    )


def make_mix(group, exchanges, rows, model_width, capacity):
    def kernel(me_ref, *refs):
        pieces, (slot, out) = refs[:-2], refs[-2:]
        me = me_ref[0]
        where = slot[:, 0:1]
        per = len(pieces) // 2
        first = functools.reduce(
            jnp.logical_or, [me == target for _, target in exchanges[0][0]]
        )
        total = None
        for j in range(per):
            piece = jnp.where(
                lax.broadcasted_iota(I32, (capacity, model_width), 0) * 0 + first.astype(I32) > 0,
                pieces[j][...].astype(F32),
                pieces[per + j][...].astype(F32),
            ).astype(BF16)
            turn = jnp.zeros_like(me)
            if j < per - 1:
                for exchange in exchanges:
                    for source, target in exchange[j]:
                        turn = jnp.where(me == target, (source - target) % group, turn)
            place = lax.broadcasted_iota(I32, (rows, capacity), 1) + turn * capacity
            pick = jnp.where(place == where, 1.0, 0.0).astype(BF16)
            term = jnp.dot(pick, piece, preferred_element_type=F32)
            total = term if total is None else total + term
        out[...] = total.astype(BF16)

    return pl.pallas_call(
        kernel,
        out_shape=jax.ShapeDtypeStruct((rows, model_width), BF16),
        in_specs=[SMEM_SPEC] + [VMEM_SPEC] * (2 * (len(exchanges[0]) + 1) + 1),
        out_specs=VMEM_SPEC,
        compiler_params=limit(16),
        cost_estimate=cost(4 * rows * rows * model_width, 8 * rows * model_width),
        name="mix",
    )


BATCHES = ((0, 3), (1, 2))
HOMEWARD = (
    (((1, 0), (2, 3)), ((2, 0), (1, 3)), ((3, 0), (0, 3))),
    (((3, 1), (0, 2)), ((0, 1), (3, 2)), ((2, 1), (1, 2))),
)


def by_heads(
    item_ids, domains, live_counts, table, norm_gains, proj_in, proj_out, expert_in, expert_out
):
    group = lax.axis_size("emb")
    me = lax.axis_index("emb").astype(I32)[None]
    rows = domains.shape[0]
    model_width = proj_out.shape[0]
    hidden_units = expert_out.shape[1]
    width = model_width // group
    capacity = 2 * rows // group
    ends = [round(group * sum(CHUNKS[: c + 1])) for c in range(len(CHUNKS))]
    chunks = list(zip([0, *ends[:-1]], ends))

    high = lax.div(live_counts[0], TAIL)
    tail = jnp.arange(TAIL, dtype=I32) < TAIL - 1
    tail = jnp.where(tail, high, live_counts[0] - high * TAIL).astype(BF16)
    count_code = jnp.broadcast_to(tail[:, None], (TAIL, width))
    domain_code = jnp.pad(
        domains.reshape(rows // width, width), ((0, TAIL - rows // width), (0, 0))
    ).astype(BF16)
    cut = chunks[0][1] * rows
    fetch = lambda ids: table.at[ids].get(mode="promise_in_bounds", wrap_negative_indices=False)
    opening = jnp.concatenate((fetch(item_ids[:cut]), count_code))
    rest = fetch(item_ids[cut:])
    mine = [opening, jnp.concatenate((rest, domain_code))]
    low, high, far = [], [], []
    for c, piece in enumerate(mine):
        low.append(rotated(piece, "emb", 1))
        high.append(rotated(piece, "emb", -1))
        far.append(rotated(low[c], "emb", 1))

    weights = make_weights(model_width, width)(me, proj_in, proj_in, proj_in)
    queries, own, before, after, embedded = [], [], [], [], []
    lives = acc = None
    for c, blocks in enumerate(chunks):
        project = make_project(group, blocks, rows, width, model_width)
        known = () if c == 0 else (lives,)
        pieces = (mine[c], low[c], high[c], far[c])
        q, kv, emb, *more = project(me, *known, *pieces, norm_gains, weights)
        if c == 0:
            lives = more[0]
        queries.append(q)
        own.append(kv)
        embedded.append(emb)
        before.append(shifted(kv, "seq", 1))
        after.append(shifted(kv, "seq", -1))
        if c == len(chunks) - 2:
            acc, q_all = make_own(chunks, True, rows, width)(lives, *queries, *own)
    for c in range(len(chunks) - 1):
        heads = () if c == 0 else (before[0], after[0])
        acc = make_near(c, chunks, rows, width)(before[c], after[c], *heads, q_all, acc)
    acc, q_all = make_own(chunks, False, rows, width)(lives, q_all, queries[-1], *own, acc)

    slots, slot_col = make_slots(group, mine[1].shape[0] - TAIL, rows, capacity)(
        me, lives, mine[1], low[1], high[1], far[1]
    )
    sent = []
    for batch in BATCHES:
        last = make_last(batch, chunks, rows, width, capacity)
        shares = last(*after, before[-1], before[0], q_all, acc, slots)
        arrived = [shares[0]]
        for k in range(1, group):
            arrived.append(rotated(shares[k], "emb", k))
        sent.append(arrived)
    finished = []
    for n, batch in enumerate(BATCHES):
        homes, select = make_select(batch, chunks, rows, model_width, capacity)
        emb, gating = select(*(embedded[h] for h in homes), slots, norm_gains, proj_in)
        senders = [source for pairs in HOMEWARD[n] for source, target in pairs[:1]]
        serve = make_serve(batch, senders, group, width, model_width, hidden_units, capacity)
        made = serve(
            me, *sent[n], emb, gating, norm_gains, proj_out, expert_in, expert_out
        )
        for j, pairs in enumerate(HOMEWARD[n]):
            finished.append(lax.ppermute(made[j], "emb", pairs))
        finished.append(made[-1])
    mix = make_mix(group, HOMEWARD, rows, model_width, capacity)
    return mix(me, *finished, slot_col)


def by_rows(
    item_ids, domains, live_counts, table, norm_gains, proj_in, proj_out, expert_in, expert_out
):
    rows_dev = domains.shape[0]
    model_width = proj_out.shape[0]
    hidden_units = expert_out.shape[1]
    group_size = lax.axis_size("emb")
    capacity = 2 * rows_dev // group_size
    columns = table[item_ids]
    embedded = lax.all_to_all(columns, "emb", split_axis=0, concat_axis=1, tiled=True).astype(
        jnp.float32
    )
    positions = jnp.arange(rows_dev, dtype=jnp.int32)
    live_mask = (positions < live_counts[0]).astype(jnp.float32)
    normed = (rms_norm(embedded, norm_gains[0]) * live_mask[:, None]).astype(jnp.bfloat16)
    projected = jnp.dot(normed, proj_in, preferred_element_type=jnp.float32)
    gating = jax.nn.silu(projected[:, :model_width])
    queries = (
        projected[:, model_width : 2 * model_width]
        .astype(jnp.bfloat16)
        .reshape(rows_dev, HEADS, HEAD_DIM)
    )
    own_pair = jnp.stack(
        (
            projected[:, 2 * model_width : 3 * model_width].astype(jnp.bfloat16),
            projected[:, 3 * model_width :].astype(jnp.bfloat16),
        )
    )
    key_weights = proj_in[:, 2 * model_width :]
    upper_band = positions[None, :] >= positions[:, None]
    lower_band = positions[None, :] <= positions[:, None]
    score_scale = 1.0 / math.sqrt(HEAD_DIM)

    def unpack(piece):
        rebuilt = jnp.dot(piece[0], key_weights, preferred_element_type=jnp.float32)
        return jnp.stack(
            (
                rebuilt[:, :model_width].astype(jnp.bfloat16),
                rebuilt[:, model_width:].astype(jnp.bfloat16),
            )
        )

    def attend(both, band_mask):
        key_heads = both[0].reshape(rows_dev, HEADS, HEAD_DIM)
        value_heads = both[1].reshape(rows_dev, HEADS, HEAD_DIM)
        scores = (
            jnp.einsum("qhd,khd->hqk", queries, key_heads, preferred_element_type=jnp.float32)
            * score_scale
        )
        weights = jax.nn.silu(scores)
        if band_mask is not None:
            weights = jnp.where(band_mask[None], weights, 0.0)
        weights = weights.astype(jnp.bfloat16)
        return jnp.einsum(
            "hqk,khd->qhd", weights, value_heads, preferred_element_type=jnp.float32
        ).reshape(rows_dev, model_width)

    outgoing = normed[None]
    attended = attend(own_pair, None)
    for distance in range(1, SPAN + 1):
        band_before = upper_band if distance == SPAN else None
        band_after = lower_band if distance == SPAN else None
        earlier = shifted(outgoing, ("seq", "emb"), distance)
        following = shifted(outgoing, ("seq", "emb"), -distance)
        attended = (
            attended + attend(unpack(earlier), band_before) + attend(unpack(following), band_after)
        )
    gated = (rms_norm(attended, norm_gains[1]) * gating).astype(jnp.bfloat16)
    hidden = embedded + jnp.dot(gated, proj_out, preferred_element_type=jnp.float32)
    routed = rms_norm(hidden, norm_gains[2]).astype(jnp.bfloat16)
    onehot_domain = (domains[:, None] == jnp.arange(group_size, dtype=jnp.int32)[None, :]).astype(
        jnp.int32
    )
    slot_rank = jnp.sum((jnp.cumsum(onehot_domain, axis=0) - onehot_domain) * onehot_domain, axis=1)
    slot_index = domains * capacity + slot_rank
    outgoing_rows = (
        jnp.zeros((group_size * capacity, model_width), jnp.bfloat16).at[slot_index].set(routed)
    )
    outgoing_rows = outgoing_rows.reshape(group_size, capacity, model_width)
    inbox = lax.all_to_all(outgoing_rows, "emb", split_axis=0, concat_axis=0, tiled=True)
    sources, slot_count, _ = inbox.shape
    flattened = inbox.reshape(sources * slot_count, model_width)
    gate_up = jnp.dot(flattened, expert_in[0], preferred_element_type=jnp.float32)
    activated = (jax.nn.silu(gate_up[:, :hidden_units]) * gate_up[:, hidden_units:]).astype(
        jnp.bfloat16
    )
    produced = jnp.dot(activated, expert_out[0], preferred_element_type=jnp.float32).astype(
        jnp.bfloat16
    )
    finished = produced.reshape(sources, slot_count, model_width)
    returned = lax.all_to_all(finished, "emb", split_axis=0, concat_axis=0, tiled=True).reshape(
        group_size * capacity, model_width
    )
    expert_rows = returned[slot_index].astype(jnp.float32)
    return (live_mask[:, None] * (hidden + expert_rows)).astype(jnp.bfloat16)


def solution(mesh):
    group = mesh.shape["emb"]
    split_heads = group == SPAN and HEADS == 2 * group

    def body(*arrays):
        return (by_heads if split_heads else by_rows)(*arrays)

    in_specs = (
        P("seq"),
        P(("seq", "emb")),
        P(("seq", "emb")),
        P(None, "emb"),
        P(),
        P(),
        P(),
        P("emb", None, None),
        P("emb", None, None),
    )
    out_specs = P(("seq", "emb"), None)
    return jax.shard_map(body, mesh=mesh, in_specs=in_specs, out_specs=out_specs, check_vma=False)
```
